256 devices in a mesh: patch: 32 (over x, y, z_lo), shard: 8 (over z_hi, core).
Axes of the slice: x: 4, y: 4, z: 8 (z_hi: 4, z_lo: 2; z = z_hi * 2 + z_lo), core: 2. Of those that a mesh axis runs over, the one named last changes fastest.
Arguments:
- node_latent: bfloat16 [32768, 512], P(('patch', 'shard')), may hold values from -6 to 6
- edge_latent: bfloat16 [262144, 512], P(('patch', 'shard')), may hold values from -6 to 6
- senders: int32 [262144], P(('patch', 'shard')), may hold values from 0 to 1535
- receivers: int32 [262144], P(('patch', 'shard')), may hold values from 0 to 1023
- halo_list: int32 [32, 512], P('patch'), may hold values from 0 to 1023
- w_edge_first: bfloat16 [1536, 512], replicated, may hold values from -0.15625 to 0.15625
- w_edge_second: bfloat16 [512, 512], replicated, may hold values from -0.25 to 0.25
- w_node_first: bfloat16 [1024, 512], replicated, may hold values from -0.1875 to 0.1875
- w_node_second: bfloat16 [512, 512], replicated, may hold values from -0.25 to 0.25
- grad_node_new: bfloat16 [32768, 512], P(('patch', 'shard')), may hold values from -24 to 24
- grad_edge_new: bfloat16 [262144, 512], P(('patch', 'shard')), may hold values from -24 to 24
Outputs:
- grad_node_latent: bfloat16 [32768, 512], P(('patch', 'shard'))
- grad_edge_latent: bfloat16 [262144, 512], P(('patch', 'shard'))
- grad_edge_first: float32 [1536, 512], P(None, 'patch')
- grad_edge_second: float32 [512, 512], P(None, 'patch')
- grad_node_first: float32 [1024, 512], P(None, 'patch')
- grad_node_second: float32 [512, 512], P(None, 'patch')
The draws below stay inside these ranges and needn't reach their ends.
All inputs are finite; a program needn't handle non-finite values.
Results may differ from the reference program's by a relative error of at most 0.03.
Values may be sent and summed in bfloat16 or wider, within the bound.
No kernel may reach another device: no remote copies, remote signals or barrier semaphores. Data moves between devices by JAX's collectives and lax.ppermute only.
A program may use at most 128 MiB of HBM per device.

```python
import jax
import jax.numpy as jnp
from jax import lax

D = 512
UNITS = 512
EDGE_DEV = 1024
NODE_DEV = 128
PATCH_NODES = 1024
HALO = 256
NODES = 32768
EDGES = 262144
N_PATCH = 32
N_SHARD = 8


def plant(values, rng, smallest, top_value):
    longest = values.shape.index(max(values.shape))
    spots = []
    for shift in (0, 1):
        where = [jax.random.randint(jax.random.fold_in(rng, axis), (), 0, length) for axis, length in enumerate(values.shape)]
        where[longest] = (where[longest] + shift) % values.shape[longest]
        spots.append(tuple(where))
    return values.at[spots[0]].set(smallest).at[spots[1]].set(top_value)


def spiked(drawn, stream_key, source, target, shards_of, factor):
    owner, partner = [(jnp.arange(drawn.shape[axis_at]) // (drawn.shape[axis_at] // shards_of)).reshape([-1 if axis == axis_at else 1 for axis in range(drawn.ndim)]) for axis_at in (source, target)]
    chosen = jax.random.permutation(stream_key, shards_of)[partner]
    strong = (owner == chosen) | (owner == (partner + shards_of // 2) % shards_of)
    return jnp.where(strong, factor * drawn, drawn)


def shard_levels(key, extent, split, smallest, largest):
    level = 1.0
    for dim, blocks in split:
        draws = jax.random.uniform(jax.random.fold_in(jax.random.fold_in(key, 6), dim), (blocks,), jnp.float32, smallest / len(split), largest / len(split))
        level = level * jnp.repeat(jnp.exp(draws), extent[dim] // blocks).reshape((-1,) + (1,) * (len(extent) - 1 - dim))
    return level


def bell_draw(key, dims, spread, limit, pieces=(), dtype=jnp.bfloat16):
    gain = shard_levels(key, dims, pieces, -0.22, 0.18) if pieces else 1.0
    drawn = jax.random.normal(key, dims, jnp.float32) * spread * gain
    return jnp.minimum(jnp.maximum(drawn, -limit), limit).astype(dtype)


def heavy_noise(own_key, dims, spread, bound, pieces, heavy, dtype=jnp.bfloat16):
    entries = spread * jax.random.normal(own_key, dims, jnp.float32)
    if pieces:
        entries = entries * shard_levels(own_key, dims, pieces, -0.22, 0.18)
    return jnp.clip(spiked(entries, jax.random.fold_in(own_key, 3), *heavy), -bound, bound).astype(dtype)


def setup_inputs(seed: int = 0) -> dict:
    streams_of = jax.random.split(jax.random.key(seed), 12)
    node_latent = bell_draw(streams_of[0], (NODES, D), 1.0, 6.0, ((0, 256),))
    edge_latent = bell_draw(streams_of[1], (EDGES, D), 1.0, 6.0, ((0, 256),))
    senders = plant(jax.random.randint(streams_of[2], (EDGES,), 0, PATCH_NODES + 2 * HALO), jax.random.fold_in(streams_of[2], 1), 0, (PATCH_NODES + 2 * HALO) - 1).astype(jnp.int32)
    receivers = plant(jax.random.randint(streams_of[3], (EDGES,), 0, PATCH_NODES), jax.random.fold_in(streams_of[3], 1), 0, PATCH_NODES - 1).astype(jnp.int32)
    halo_list = plant(jax.random.randint(streams_of[4], (N_PATCH, 2 * HALO), 0, PATCH_NODES), jax.random.fold_in(streams_of[4], 1), 0, PATCH_NODES - 1).astype(jnp.int32)
    w_edge_first = bell_draw(streams_of[5], (3 * D, UNITS), (3 * D) ** -0.5, 0.15625)
    w_edge_second = bell_draw(streams_of[6], (UNITS, D), UNITS ** -0.5, 0.25)
    w_node_first = bell_draw(streams_of[7], (2 * D, UNITS), (2 * D) ** -0.5, 0.1875)
    w_node_second = bell_draw(streams_of[8], (UNITS, D), UNITS ** -0.5, 0.25)
    grad_node_new = heavy_noise(streams_of[9], (NODES, D), 1.0, 24.0, ((0, 256),), (0, 1, 256, 6.0))
    grad_edge_new = heavy_noise(streams_of[10], (EDGES, D), 1.0, 24.0, ((0, 256),), (0, 1, 256, 6.0))
    return dict(node_latent=node_latent, edge_latent=edge_latent, senders=senders, receivers=receivers, halo_list=halo_list, w_edge_first=w_edge_first, w_edge_second=w_edge_second, w_node_first=w_node_first, w_node_second=w_node_second, grad_node_new=grad_node_new, grad_edge_new=grad_edge_new)


epsilon = 1e-05

def swish_slope(values):
    sig = jax.nn.sigmoid(values)
    return sig * (1.0 + values * (1.0 - sig))

def contract_rows(left, right):
    return lax.dot_general(left, right, (((0,), (0,)), ((), ())), preferred_element_type=jnp.float32)

def times_transpose(left, right):
    return lax.dot_general(left, right, (((1,), (1,)), ((), ())), preferred_element_type=jnp.float32)

def mlp_forward(joined, w_first, w_second):
    pre_act = jnp.dot(joined, w_first, preferred_element_type=jnp.float32)
    activated = (pre_act * jax.nn.sigmoid(pre_act)).astype(jnp.bfloat16)
    output = jnp.dot(activated, w_second, preferred_element_type=jnp.float32)
    center = output - lax.optimization_barrier(jnp.mean(output, axis=-1, keepdims=True))
    inv_scale = lax.rsqrt(lax.optimization_barrier(jnp.mean(center * center, axis=-1, keepdims=True)) + epsilon)
    return (pre_act, activated, center * inv_scale, inv_scale)

def mlp_backward(joined, w_first, w_second, pre_act, activated, normed, inv_scale, cotangent):
    d_out = inv_scale * (cotangent - lax.optimization_barrier(jnp.mean(cotangent, axis=-1, keepdims=True)) - normed * lax.optimization_barrier(jnp.mean(cotangent * normed, axis=-1, keepdims=True)))
    d_out = d_out.astype(jnp.bfloat16)
    d_act = times_transpose(d_out, w_second)
    d_pre = (d_act * swish_slope(pre_act)).astype(jnp.bfloat16)
    grad_second = contract_rows(activated, d_out)
    grad_first = contract_rows(joined, d_pre)
    d_joined = times_transpose(d_pre, w_first)
    return (d_joined, grad_first, grad_second)

def reference(node_latent, edge_latent, senders, receivers, halo_list, w_edge_first, w_edge_second, w_node_first, w_node_second, grad_node_new, grad_edge_new):
    patch_rows = NODE_DEV * N_SHARD
    patch_edges = EDGE_DEV * N_SHARD
    nodes_all = node_latent.reshape(N_PATCH, patch_rows, D)
    outgoing = jax.vmap(lambda tab, idx: jnp.take(tab, idx, axis=0))(nodes_all, halo_list)
    from_prev = jnp.roll(outgoing[:, HALO:], 1, axis=0)
    from_next = jnp.roll(outgoing[:, :HALO], -1, axis=0)
    tables = jnp.concatenate([from_prev, nodes_all, from_next], axis=1)

    def one_patch(carry, items):
        table, own_nodes, edges, send_idx, recv_idx, node_cot, edge_cot = items
        joined = jnp.concatenate([edges, jnp.take(table, send_idx, axis=0), jnp.take(own_nodes, recv_idx, axis=0)], axis=1)
        pre_act, activated, normed, inv_scale = mlp_forward(joined, w_edge_first, w_edge_second)
        edge_new = (edges.astype(jnp.float32) + normed).astype(jnp.bfloat16)
        aggregate = jax.ops.segment_sum(edge_new.astype(jnp.float32), recv_idx, num_segments=patch_rows).astype(jnp.bfloat16)
        node_joined = jnp.concatenate([own_nodes, aggregate], axis=1)
        n_pre, n_act, n_normed, n_inv = mlp_forward(node_joined, w_node_first, w_node_second)
        node_grad = node_cot.astype(jnp.float32)
        d_node, g_node_first, g_node_second = mlp_backward(node_joined, w_node_first, w_node_second, n_pre, n_act, n_normed, n_inv, node_grad)
        d_aggregate = d_node[:, D:]
        edge_grad = edge_cot.astype(jnp.float32) + jnp.take(d_aggregate, recv_idx, axis=0)
        d_edge, g_edge_first, g_edge_second = mlp_backward(joined, w_edge_first, w_edge_second, pre_act, activated, normed, inv_scale, edge_grad)
        grad_edges = (edge_grad + d_edge[:, :D]).astype(jnp.bfloat16)
        sender_part = jax.ops.segment_sum(d_edge[:, D:2 * D], send_idx, num_segments=patch_rows + 2 * HALO)
        receiver_part = jax.ops.segment_sum(d_edge[:, 2 * D:], recv_idx, num_segments=patch_rows)
        own_part = sender_part[HALO:HALO + patch_rows] + receiver_part + node_grad + d_node[:, :D]
        back_part = jnp.concatenate([sender_part[:HALO], sender_part[HALO + patch_rows:]], axis=0)
        carry = (carry[0] + g_edge_first, carry[1] + g_edge_second, carry[2] + g_node_first, carry[3] + g_node_second)
        return (carry, (grad_edges, own_part, back_part))
    start = (jnp.zeros((3 * D, UNITS), jnp.float32), jnp.zeros((UNITS, D), jnp.float32), jnp.zeros((2 * D, UNITS), jnp.float32), jnp.zeros((UNITS, D), jnp.float32))
    items = (tables, nodes_all, edge_latent.reshape(N_PATCH, patch_edges, D), senders.reshape(N_PATCH, patch_edges), receivers.reshape(N_PATCH, patch_edges), grad_node_new.reshape(N_PATCH, patch_rows, D), grad_edge_new.reshape(N_PATCH, patch_edges, D))
    sums, (grad_edges, own_parts, back_parts) = lax.scan(one_patch, start, items)
    recv_prev = jnp.roll(back_parts[:, HALO:], 1, axis=0)
    recv_next = jnp.roll(back_parts[:, :HALO], -1, axis=0)

    def add_back(own_part, idx, got_prev, got_next):
        return own_part.at[idx[:HALO]].add(got_prev).at[idx[HALO:]].add(got_next)
    own_parts = jax.vmap(add_back)(own_parts, halo_list, recv_prev, recv_next)
    grad_node_latent = own_parts.reshape(N_PATCH * patch_rows, D).astype(jnp.bfloat16)
    grad_edge_latent = grad_edges.reshape(N_PATCH * patch_edges, D)
    return (grad_node_latent, grad_edge_latent, sums[0], sums[1], sums[2], sums[3])
```

```python
import functools

import jax
import jax.numpy as jnp
from jax import lax
from jax.experimental import pallas as pl
from jax.experimental.pallas import tpu as pltpu
from jax.sharding import PartitionSpec as P

epsilon = 1e-05
F32 = jnp.float32
BF16 = jnp.bfloat16
MIB = 1 << 20


def over_ring(x, by):
    count = lax.axis_size("shard")
    return lax.ppermute(x, "shard", [(i, (i + 2 * by) % count) for i in range(count)])


def to_partner(x):
    count = lax.axis_size("shard")
    return lax.ppermute(x, "shard", [(i, i ^ 1) for i in range(count)])


def to_patch(x, by):
    count = lax.axis_size("patch")
    return lax.ppermute(x, "patch", [(i, (i + by) % count) for i in range(count)])


def spread_over_shard(own):
    after = over_ring(own, -1)
    before = over_ring(own, 1)
    across = over_ring(own, 2)
    mine = [own, after, across, before]
    return mine + [to_partner(b) for b in mine]


def ring_sum_parts(chunks):
    return [over_ring(chunks[0], 1), over_ring(chunks[1], 2), over_ring(chunks[2], -1)]


def dot(a, b):
    return jnp.dot(a, b, preferred_element_type=F32)


def dot_nt(a, b):
    return lax.dot_general(a, b, (((1,), (1,)), ((), ())), preferred_element_type=F32)


def dot_tn(a, b):
    return lax.dot_general(a, b, (((0,), (0,)), ((), ())), preferred_element_type=F32)


def pick_rows(index_column, count, first=0):
    places = lax.broadcasted_iota(jnp.int32, (index_column.shape[0], count), 1) + first
    return jnp.where(places == index_column, 1.0, 0.0).astype(BF16)


def add_rows(index_row, count, first=0):
    places = lax.broadcasted_iota(jnp.int32, (count, index_row.shape[1]), 0) + first
    return jnp.where(places == index_row, 1.0, 0.0).astype(BF16)


def normalised(out):
    center = out - jnp.mean(out, axis=-1, keepdims=True)
    inv = lax.rsqrt(jnp.mean(center * center, axis=-1, keepdims=True) + epsilon)
    return center * inv, inv


def norm_backward(g, normed, inv):
    d = inv * (
        g
        - jnp.mean(g, axis=-1, keepdims=True)
        - normed * jnp.mean(g * normed, axis=-1, keepdims=True)
    )
    return d.astype(BF16)


def call(kernel, out_shapes, args, *, grid=None, in_specs=None, out_specs=None, scratch=(),
         flops=0, moved=0, vmem=32 * MIB):
    extra = {}
    if grid is not None:
        extra = dict(grid=grid, in_specs=in_specs, out_specs=out_specs)
    else:
        full = pl.BlockSpec(memory_space=pltpu.VMEM)
        extra = dict(in_specs=in_specs or [full] * len(args), out_specs=[full] * len(out_shapes))
    return pl.pallas_call(
        kernel,
        out_shape=out_shapes,
        scratch_shapes=list(scratch),
        compiler_params=pltpu.CompilerParams(vmem_limit_bytes=vmem),
        cost_estimate=pl.CostEstimate(flops=flops, bytes_accessed=moved, transcendentals=0),
        **extra,
    )(*args)


def shape(dims, dtype):
    return jax.ShapeDtypeStruct(dims, dtype)


def halo_rows_kernel(index, *refs):
    blocks, (low, high) = refs[:-2], refs[-2:]
    total = None
    for k, block in enumerate(blocks):
        part = dot(pick_rows(index[...], 128, 128 * k), block[...])
        total = part if total is None else total + part
    low[...] = total[:128].astype(BF16)
    high[...] = total[128:].astype(BF16)


def edge_forward_kernel(n_blocks, s_col, r_col, r_row, edge, *refs):
    blocks = refs[:n_blocks]
    (w1, w2, from_s, from_r, act_o, slope_o, normed_o, inv_o, keep_o, send_o, table, total) = refs[
        n_blocks:
    ]
    step = pl.program_id(0)

    @pl.when(step == 0)
    def _():
        for k, block in enumerate(blocks):
            table[pl.ds(128 * k, 128), :] = block[...]
        total[...] = jnp.zeros_like(total)

    rows_s = dot(pick_rows(s_col[...], 1536), table[...]).astype(BF16)
    rows_r = dot(pick_rows(r_col[...], 1024), table[pl.ds(0, 1024), :]).astype(BF16)
    from_s[...] = rows_s
    from_r[...] = rows_r
    pre = (
        dot(edge[...], w1[pl.ds(0, 512), :])
        + dot(rows_s, w1[pl.ds(512, 512), :])
        + dot(rows_r, w1[pl.ds(1024, 512), :])
    )
    sig = jax.nn.sigmoid(pre)
    act = (pre * sig).astype(BF16)
    act_o[...] = act
    slope_o[...] = sig * (1.0 + pre * (1.0 - sig))
    normed, inv = normalised(dot(act, w2[...]))
    normed_o[...] = normed
    inv_o[...] = inv
    edge_new = (edge[...].astype(F32) + normed).astype(BF16)
    total[...] += dot(add_rows(r_row[...], 1024), edge_new)

    @pl.when(step == pl.num_programs(0) - 1)
    def _():
        keep_o[...] = total[pl.ds(0, 512), :]
        send_o[...] = total[pl.ds(512, 512), :].astype(BF16)


def pair_sum_kernel(keep, came, own, one, two, three):
    both = keep[...] + came[...].astype(F32)
    own[...] = both[0:128]
    one[...] = both[128:256].astype(BF16)
    two[...] = both[256:384].astype(BF16)
    three[...] = both[384:512].astype(BF16)


def node_kernel(core, own, got1, got2, got3, node, grad, w1, w2, d_agg_o, part_o, keep_o, send_o, agg_s, act_s):
    agg = (
        own[...] + got1[...].astype(F32) + got2[...].astype(F32) + got3[...].astype(F32)
    ).astype(BF16)
    x = node[...]
    pre = dot(x, w1[pl.ds(0, 512), :]) + dot(agg, w1[pl.ds(512, 512), :])
    sig = jax.nn.sigmoid(pre)
    act = (pre * sig).astype(BF16)
    normed, inv = normalised(dot(act, w2[...]))
    g = grad[...].astype(F32)
    d_out = norm_backward(g, normed, inv)
    d_act = dot_nt(d_out, w2[...])
    d_pre = (d_act * (sig * (1.0 + pre * (1.0 - sig)))).astype(BF16)
    d_agg_o[...] = dot_nt(d_pre, w1[pl.ds(512, 512), :]).astype(BF16)
    part_o[...] = g + dot_nt(d_pre, w1[pl.ds(0, 512), :])
    agg_s[...] = agg
    act_s[...] = act
    mine = pl.multiple_of(core[0] * 256, 256)
    theirs = pl.multiple_of(256 - core[0] * 256, 256)
    for k, (left, right) in enumerate(((d_pre, node), (d_pre, agg_s), (d_out, act_s))):
        keep_o[:, pl.ds(256 * k, 256)] = dot_tn(left, right[:, pl.ds(mine, 256)])
        send_o[:, pl.ds(256 * k, 256)] = dot_tn(left, right[:, pl.ds(theirs, 256)]).astype(BF16)


def edge_backward_kernel(n_blocks, r_col, s_row, grad, normed, inv, slope, *refs):
    blocks = refs[:n_blocks]
    (w1, w2, d_out_o, d_pre_o, dxs_o, grad_o, keep_o, send_o, table, total) = refs[n_blocks:]
    step = pl.program_id(0)

    @pl.when(step == 0)
    def _():
        for k, block in enumerate(blocks):
            table[pl.ds(128 * k, 128), :] = block[...]
        total[...] = jnp.zeros_like(total)

    g = grad[...].astype(F32) + dot(pick_rows(r_col[...], 1024), table[...])
    d_out = norm_backward(g, normed[...], inv[...])
    d_out_o[...] = d_out
    d_pre = (dot_nt(d_out, w2[...]) * slope[...]).astype(BF16)
    d_pre_o[...] = d_pre
    dxs = dot_nt(d_pre, w1[pl.ds(512, 512), :]).astype(BF16)
    dxs_o[...] = dxs
    total[...] += dot(add_rows(s_row[...], 512, 1024), dxs)
    grad_o[...] = (g + dot_nt(d_pre, w1[pl.ds(0, 512), :])).astype(BF16)

    @pl.when(step == pl.num_programs(0) - 1)
    def _():
        keep_o[pl.ds(0, 128), :] = total[pl.ds(0, 128), :]
        keep_o[pl.ds(128, 128), :] = total[pl.ds(256, 128), :]
        send_o[pl.ds(0, 128), :] = total[pl.ds(128, 128), :].astype(BF16)
        send_o[pl.ds(128, 128), :] = total[pl.ds(384, 128), :].astype(BF16)


def edge_weights_kernel(core, d_pre, d_out, edge, from_s, from_r, act, keep_o, send_o):
    mine = pl.multiple_of(core[0] * 256, 256)
    theirs = pl.multiple_of(256 - core[0] * 256, 256)
    for k, (left, right) in enumerate(
        ((d_pre, edge), (d_pre, from_s), (d_pre, from_r), (d_out, act))
    ):
        keep_o[:, pl.ds(256 * k, 256)] = dot_tn(left[...], right[:, pl.ds(mine, 256)])
        send_o[:, pl.ds(256 * k, 256)] = dot_tn(
            left[...], right[:, pl.ds(theirs, 256)]
        ).astype(BF16)


def node_sums_kernel(s_row, r_row, d_pre, dxs, w_r, out, dxr):
    dxr[...] = dot_nt(d_pre[...], w_r[...]).astype(BF16)
    for k in range(4):
        out[pl.ds(256 * k, 256), :] = dot(add_rows(s_row[...], 256, 256 * k), dxs[...]) + dot(
            add_rows(r_row[...], 256, 256 * k), dxr[...]
        )


def pair_add_kernel(keep, came, low, high):
    both = keep[...] + came[...].astype(F32)
    low[...] = both[:128].astype(BF16)
    high[...] = both[128:].astype(BF16)


def returned_kernel(index, sums, low, high, keep_o, send_o):
    for k in range(4):
        rows = (
            sums[pl.ds(256 * k, 256), :]
            + dot(add_rows(index[:, pl.ds(0, 128)], 256, 256 * k), low[...])
            + dot(add_rows(index[:, pl.ds(128, 128)], 256, 256 * k), high[...])
        )
        if k < 2:
            keep_o[pl.ds(256 * k, 256), :] = rows
        else:
            send_o[pl.ds(256 * (k - 2), 256), :] = rows.astype(BF16)


def node_total_kernel(own, got1, got2, got3, part, out):
    out[...] = (
        own[...]
        + got1[...].astype(F32)
        + got2[...].astype(F32)
        + got3[...].astype(F32)
        + part[...]
    ).astype(BF16)


def weight_sum(keep, came):
    patches = lax.axis_size("patch")
    both = (keep + came.astype(F32)).astype(BF16)
    units, lanes = both.shape
    blocks = lax.all_to_all(
        both.reshape(patches, units // patches, lanes), "patch", 0, 0, tiled=True
    )
    return jnp.sum(blocks.astype(F32), axis=0)


def body(
    node_latent,
    edge_latent,
    senders,
    receivers,
    halo_list,
    w_edge_first,
    w_edge_second,
    w_node_first,
    w_node_second,
    grad_node_new,
    grad_edge_new,
):
    place = lax.axis_index("shard")
    core = place & 1
    chip = place >> 1

    table_blocks = spread_over_shard(node_latent)

    def relative(n):
        return (((n >> 7) & 1) ^ core) * 512 + (((n >> 8) - chip) & 3) * 128 + (n & 127)

    s_index = jnp.where(
        senders < 256,
        1024 + ((senders >> 7) ^ core) * 128 + (senders & 127),
        jnp.where(
            senders >= 1280,
            1280 + (((senders - 1280) >> 7) ^ core) * 128 + (senders & 127),
            relative(senders - 256),
        ),
    )
    r_index = relative(receivers)
    listed = relative(halo_list[0])
    half = jnp.concatenate(
        [
            lax.dynamic_slice(listed, (core * 128,), (128,)),
            lax.dynamic_slice(listed, (256 + core * 128,), (128,)),
        ]
    )
    s_col, s_row = s_index.reshape(1024, 1), s_index.reshape(1, 1024)
    r_col, r_row = r_index.reshape(1024, 1), r_index.reshape(1, 1024)
    core_word = core.reshape(1).astype(jnp.int32)

    to_prev, to_next = call(
        halo_rows_kernel,
        [shape((128, 512), BF16)] * 2,
        [half.reshape(256, 1)] + table_blocks,
        flops=2 * 256 * 1024 * 512,
        moved=2 * MIB,
        vmem=8 * MIB,
    )
    prev_mine = to_patch(to_next, 1)
    next_mine = to_patch(to_prev, -1)
    halo_blocks = [prev_mine, to_partner(prev_mine), next_mine, to_partner(next_mine)]

    tile = 256
    steps = 1024 // tile
    rows = lambda lanes: pl.BlockSpec((tile, lanes), lambda i: (i, 0))
    lanes_row = pl.BlockSpec((1, tile), lambda i: (0, i))
    fixed = lambda a, b: pl.BlockSpec((a, b), lambda i: (0, 0))
    from_s, from_r, act, slope, normed, inv, agg_keep, agg_send = call(
        functools.partial(edge_forward_kernel, 12),
        [
            shape((1024, 512), BF16),
            shape((1024, 512), BF16),
            shape((1024, 512), BF16),
            shape((1024, 512), F32),
            shape((1024, 512), F32),
            shape((1024, 1), F32),
            shape((512, 512), F32),
            shape((512, 512), BF16),
        ],
        [s_col, r_col, r_row, edge_latent]
        + table_blocks
        + halo_blocks
        + [w_edge_first, w_edge_second],
        grid=(steps,),
        in_specs=[rows(1), rows(1), lanes_row, rows(512)]
        + [fixed(128, 512)] * 12
        + [fixed(1536, 512), fixed(512, 512)],
        out_specs=[
            rows(512),
            rows(512),
            rows(512),
            rows(512),
            rows(512),
            rows(1),
            fixed(512, 512),
            fixed(512, 512),
        ],
        scratch=[pltpu.VMEM((1536, 512), BF16), pltpu.VMEM((1024, 512), F32)],
        flops=6_000_000_000,
        moved=12 * MIB,
    )
    agg_came = to_partner(agg_send)
    agg_own, agg_1, agg_2, agg_3 = call(
        pair_sum_kernel,
        [shape((128, 512), F32)] + [shape((128, 512), BF16)] * 3,
        [agg_keep, agg_came],
        moved=2 * MIB,
        vmem=8 * MIB,
    )
    smem = pl.BlockSpec(memory_space=pltpu.SMEM)
    vmem = pl.BlockSpec(memory_space=pltpu.VMEM)
    d_agg, node_part, n_keep, n_send = call(
        node_kernel,
        [
            shape((128, 512), BF16),
            shape((128, 512), F32),
            shape((512, 768), F32),
            shape((512, 768), BF16),
        ],
        [core_word, agg_own]
        + ring_sum_parts([agg_1, agg_2, agg_3])
        + [node_latent, grad_node_new, w_node_first, w_node_second],
        in_specs=[smem] + [vmem] * 8,
        scratch=[pltpu.VMEM((128, 512), BF16), pltpu.VMEM((128, 512), BF16)],
        flops=800_000_000,
        moved=5 * MIB,
        vmem=16 * MIB,
    )
    d_blocks = spread_over_shard(d_agg)
    n_came = to_partner(n_send)
    node_rows = weight_sum(n_keep, n_came)

    d_out, d_pre, dxs, grad_edge_latent, back_keep, back_send = call(
        functools.partial(edge_backward_kernel, 8),
        [
            shape((1024, 512), BF16),
            shape((1024, 512), BF16),
            shape((1024, 512), BF16),
            shape((1024, 512), BF16),
            shape((256, 512), F32),
            shape((256, 512), BF16),
        ],
        [r_col, s_row, grad_edge_new, normed, inv, slope]
        + d_blocks
        + [w_edge_first, w_edge_second],
        grid=(steps,),
        in_specs=[rows(1), lanes_row, rows(512), rows(512), rows(1), rows(512)]
        + [fixed(128, 512)] * 8
        + [fixed(1536, 512), fixed(512, 512)],
        out_specs=[rows(512)] * 4 + [fixed(256, 512)] * 2,
        scratch=[pltpu.VMEM((1024, 512), BF16), pltpu.VMEM((512, 512), F32)],
        flops=3_300_000_000,
        moved=12 * MIB,
    )
    back_came = to_partner(back_send)
    w_keep, w_send = call(
        edge_weights_kernel,
        [shape((512, 1024), F32), shape((512, 1024), BF16)],
        [core_word, d_pre, d_out, edge_latent, from_s, from_r, act],
        in_specs=[smem] + [vmem] * 6,
        flops=2_200_000_000,
        moved=9 * MIB,
    )
    w_came = to_partner(w_send)
    back_prev, back_next = call(
        pair_add_kernel,
        [shape((128, 512), BF16)] * 2,
        [back_keep, back_came],
        moved=MIB,
        vmem=8 * MIB,
    )
    got_next = to_patch(back_prev, -1)
    got_prev = to_patch(back_next, 1)
    (sums,) = call(
        node_sums_kernel,
        [shape((1024, 512), F32)],
        [s_row, r_row, d_pre, dxs, lax.slice_in_dim(w_edge_first, 1024, 1536, axis=0)],
        scratch=[pltpu.VMEM((1024, 512), BF16)],
        flops=2_700_000_000,
        moved=5 * MIB,
    )
    edge_rows = weight_sum(w_keep, w_came)
    node_keep, node_send = call(
        returned_kernel,
        [shape((512, 512), F32), shape((512, 512), BF16)],
        [half.reshape(1, 256), sums, got_prev, got_next],
        flops=300_000_000,
        moved=4 * MIB,
        vmem=16 * MIB,
    )
    node_came = to_partner(node_send)
    t_own, t_1, t_2, t_3 = call(
        pair_sum_kernel,
        [shape((128, 512), F32)] + [shape((128, 512), BF16)] * 3,
        [node_keep, node_came],
        moved=2 * MIB,
        vmem=8 * MIB,
    )
    (grad_node_latent,) = call(
        node_total_kernel,
        [shape((128, 512), BF16)],
        [t_own] + ring_sum_parts([t_1, t_2, t_3]) + [node_part],
        moved=MIB,
        vmem=8 * MIB,
    )

    weight_rows = jnp.concatenate([edge_rows, node_rows], axis=1)
    sent = weight_rows.astype(BF16)
    for by in (1, 2, 3):
        weight_rows = weight_rows + over_ring(sent, by).astype(F32)
    other = to_partner(weight_rows.astype(BF16)).astype(F32)
    low = jnp.where(core == 0, weight_rows, other)
    high = jnp.where(core == 0, other, weight_rows)

    def joined(first, count):
        parts = []
        for k in range(first, first + count):
            parts += [low[:, 256 * k : 256 * k + 256], high[:, 256 * k : 256 * k + 256]]
        return jnp.concatenate(parts, axis=1).T

    return (
        grad_node_latent,
        grad_edge_latent,
        joined(0, 3),
        joined(3, 1),
        joined(4, 2),
        joined(6, 1),
    )


def solution(mesh):
    split = P(("patch", "shard"), None)
    ids = P(("patch", "shard"))
    in_specs = (split, split, ids, ids, P("patch", None), P(), P(), P(), P(), split, split)
    out_specs = (split, split) + (P(None, "patch"),) * 4
    return jax.shard_map(body, mesh=mesh, in_specs=in_specs, out_specs=out_specs, check_vma=False)
```

```python
import jax
import jax.numpy as jnp
from jax import lax
from jax.experimental import pallas as pl
from jax.experimental.pallas import tpu as pltpu
from jax.sharding import PartitionSpec as P


epsilon = 1e-05
F32 = jnp.float32
BF16 = jnp.bfloat16
MIB = 1 << 20


def over_ring(x, by):
    count = lax.axis_size("shard")
    return lax.ppermute(x, "shard", [(i, (i + 2 * by) % count) for i in range(count)])


def to_partner(x):
    count = lax.axis_size("shard")
    return lax.ppermute(x, "shard", [(i, i ^ 1) for i in range(count)])


def to_patch(x, by):
    count = lax.axis_size("patch")
    return lax.ppermute(x, "patch", [(i, (i + by) % count) for i in range(count)])


def spread_over_shard(own):
    across = over_ring(own, 2)
    after = over_ring(own, -1)
    before = over_ring(own, 1)
    mine = [own, after, across, before]
    return mine + [to_partner(b) for b in mine]


def ring_sum_parts(chunks):
    return [over_ring(chunks[0], 1), over_ring(chunks[1], 2), over_ring(chunks[2], -1)]


def dot(a, b):
    return jnp.dot(a, b, preferred_element_type=F32)


def dot_nt(a, b):
    return lax.dot_general(a, b, (((1,), (1,)), ((), ())), preferred_element_type=F32)


def dot_tn(a, b):
    return lax.dot_general(a, b, (((0,), (0,)), ((), ())), preferred_element_type=F32)


def pick_rows(index_column, count, first=0):
    places = lax.broadcasted_iota(jnp.int32, (index_column.shape[0], count), 1) + first
    return jnp.where(places == index_column, 1.0, 0.0).astype(BF16)


def add_rows(index_row, count, first=0):
    places = lax.broadcasted_iota(jnp.int32, (count, index_row.shape[1]), 0) + first
    return jnp.where(places == index_row, 1.0, 0.0).astype(BF16)


def normalised(out):
    center = out - jnp.mean(out, axis=-1, keepdims=True)
    inv = lax.rsqrt(jnp.mean(center * center, axis=-1, keepdims=True) + epsilon)
    return center * inv, inv


def norm_backward(g, normed, inv):
    d = inv * (
        g
        - jnp.mean(g, axis=-1, keepdims=True)
        - normed * jnp.mean(g * normed, axis=-1, keepdims=True)
    )
    return d.astype(BF16)


def call(
    kernel, out_shapes, args, *, far=(), words=(), far_out=(), scratch=(), flops=0, moved=0, vmem=16 * MIB
):
    full = pl.BlockSpec(memory_space=pltpu.VMEM)
    hbm = pl.BlockSpec(memory_space=pltpu.HBM)
    smem = pl.BlockSpec(memory_space=pltpu.SMEM)
    in_specs = [hbm if i in far else smem if i in words else full for i in range(len(args))]
    out_specs = [hbm if i in far_out else full for i in range(len(out_shapes))]
    out_shapes = [
        pltpu.HBM(o.shape, o.dtype) if i in far_out else o for i, o in enumerate(out_shapes)
    ]
    args = [
        pltpu.with_memory_space_constraint(a, pltpu.HBM) if i in far else a
        for i, a in enumerate(args)
    ]
    return pl.pallas_call(
        kernel,
        out_shape=out_shapes,
        in_specs=in_specs,
        out_specs=out_specs,
        scratch_shapes=list(scratch),
        compiler_params=pltpu.CompilerParams(vmem_limit_bytes=vmem),
        cost_estimate=pl.CostEstimate(flops=flops, bytes_accessed=moved, transcendentals=0),
    )(*args)


def shape(dims, dtype):
    return jax.ShapeDtypeStruct(dims, dtype)


def begin(src, dst, sem):
    copy = pltpu.make_async_copy(src, dst, sem)
    copy.start()
    return copy


def halo_rows_kernel(index, own, *refs):
    blocks, (low, high, held, sem) = refs[:7], refs[7:]
    arriving = begin(own, held, sem.at[0])
    total = None
    for k, block in enumerate(blocks):
        part = dot(pick_rows(index[...], 128, 128 * (k + 1)), block[...])
        total = part if total is None else total + part
    arriving.wait()
    total = total + dot(pick_rows(index[...], 128), held[...])
    low[...] = total[:128].astype(BF16)
    high[...] = total[128:].astype(BF16)


TILE = 256
TILES = 4


def tiles(body):
    lax.fori_loop(
        0, TILES, lambda i, _: (body(i, pl.ds(pl.multiple_of(i * TILE, TILE), TILE)), 0)[1], 0
    )


def edge_start_kernel(s_col, r_col, edge_h, own_h, *refs):
    blocks = refs[:7]
    (w1_h, from_s, from_r_h, pre_o, table, edge, w1, from_r, sem) = refs[7:]
    got_own = begin(own_h, table.at[pl.ds(0, 128), :], sem.at[0])
    got_w1 = begin(w1_h, w1, sem.at[1])
    got_edge = begin(edge_h, edge, sem.at[2])
    for k, block in enumerate(blocks):
        table[pl.ds(128 * (k + 1), 128), :] = block[...]
    got_own.wait()

    def gather(i, rows):
        from_s[rows, :] = dot(pick_rows(s_col[rows, :], 1024), table[...]).astype(BF16)
        from_r[rows, :] = dot(pick_rows(r_col[rows, :], 1024), table[...]).astype(BF16)
        begin(from_r.at[rows, :], from_r_h.at[rows, :], sem.at[3 + i])

    tiles(gather)
    got_w1.wait()
    got_edge.wait()

    def multiply(i, rows):
        pre_o[rows, :] = (
            dot(edge[rows, :], w1[pl.ds(0, 512), :])
            + dot(from_s[rows, :], w1[pl.ds(512, 512), :])
            + dot(from_r[rows, :], w1[pl.ds(1024, 512), :])
        )

    tiles(multiply)

    def finish(i, rows):
        pltpu.make_async_copy(from_r.at[rows, :], from_r_h.at[rows, :], sem.at[3 + i]).wait()

    tiles(finish)


def edge_forward_kernel(s_col, r_row, edge_h, from_s, pre_i, *refs):
    blocks = refs[:4]
    (w1_h, w2_h, from_s_h, act_h, slope_h, normed_h, inv_h, keep_o, send_o) = refs[4:13]
    (table, news, edge, w1, w2, from_s_o, act_o, slope_o, normed_o, inv_o, sem, out_sem) = refs[13:]
    got_w1 = begin(w1_h.at[pl.ds(512, 512), :], w1, sem.at[0])
    got_w2 = begin(w2_h, w2, sem.at[1])
    got_edge = begin(edge_h, edge, sem.at[2])
    for k, block in enumerate(blocks):
        table[pl.ds(128 * k, 128), :] = block[...]
    got_w1.wait()
    got_w2.wait()
    got_edge.wait()
    leaving = (
        (from_s_o, from_s_h),
        (act_o, act_h),
        (slope_o, slope_h),
        (normed_o, normed_h),
        (inv_o, inv_h),
    )

    def tile(i, rows):
        halo = dot(pick_rows(s_col[rows, :], 512, 1024), table[...]).astype(BF16)
        from_s_o[rows, :] = from_s[rows, :] + halo
        pre = pre_i[rows, :] + dot(halo, w1[...])
        sig = jax.nn.sigmoid(pre)
        act = (pre * sig).astype(BF16)
        act_o[rows, :] = act
        slope_o[rows, :] = sig * (1.0 + pre * (1.0 - sig))
        normed, inv = normalised(dot(act, w2[...]))
        normed_o[rows, :] = normed
        inv_o[rows, :] = inv
        news[rows, :] = (edge[rows, :].astype(F32) + normed).astype(BF16)
        for k, (here, there) in enumerate(leaving):
            begin(here.at[rows, :], there.at[rows, :], out_sem.at[k, i])

    tiles(tile)
    for k in (2, 3, 0, 1):
        sums = dot(add_rows(r_row[...], 256, 256 * k), news[...])
        if k < 2:
            keep_o[pl.ds(256 * k, 256), :] = sums
        else:
            send_o[pl.ds(256 * (k - 2), 256), :] = sums.astype(BF16)

    def finish(i, rows):
        for k, (here, there) in enumerate(leaving):
            pltpu.make_async_copy(here.at[rows, :], there.at[rows, :], out_sem.at[k, i]).wait()

    tiles(finish)


def pair_sum_kernel(keep, came, own, one, two, three):
    both = keep[...] + came[...].astype(F32)
    own[...] = both[0:128]
    one[...] = both[128:256].astype(BF16)
    two[...] = both[256:384].astype(BF16)
    three[...] = both[384:512].astype(BF16)


def node_kernel(core, own, got1, got2, got3, node, grad, w1, w2, d_agg_o, part_o, keep_o, send_o, agg_s, act_s):
    agg = (
        own[...] + got1[...].astype(F32) + got2[...].astype(F32) + got3[...].astype(F32)
    ).astype(BF16)
    x = node[...]
    pre = dot(x, w1[pl.ds(0, 512), :]) + dot(agg, w1[pl.ds(512, 512), :])
    sig = jax.nn.sigmoid(pre)
    act = (pre * sig).astype(BF16)
    normed, inv = normalised(dot(act, w2[...]))
    g = grad[...].astype(F32)
    d_out = norm_backward(g, normed, inv)
    d_act = dot_nt(d_out, w2[...])
    d_pre = (d_act * (sig * (1.0 + pre * (1.0 - sig)))).astype(BF16)
    d_agg_o[...] = dot_nt(d_pre, w1[pl.ds(512, 512), :]).astype(BF16)
    part_o[...] = g + dot_nt(d_pre, w1[pl.ds(0, 512), :])
    agg_s[...] = agg
    act_s[...] = act
    mine = pl.multiple_of(core[0] * 256, 256)
    theirs = pl.multiple_of(256 - core[0] * 256, 256)
    for k, (left, right) in enumerate(((d_pre, node), (d_pre, agg_s), (d_out, act_s))):
        keep_o[:, pl.ds(256 * k, 256)] = dot_tn(left, right[:, pl.ds(mine, 256)])
        send_o[:, pl.ds(256 * k, 256)] = dot_tn(left, right[:, pl.ds(theirs, 256)]).astype(BF16)


def edge_backward_kernel(core, r_col, s_row, grad_h, normed_h, inv_h, slope_h, edge_h, from_s_h, from_r_h, act_h, *refs):
    blocks = refs[:8]
    (w1_h, w2_h, d_pre_h, dxs_h, grad_o_h, back_keep, back_send, keep_o, send_o) = refs[8:17]
    (table, d_outs, d_pres, dxss, grad_o, grad, normed, inv, slope) = refs[17:26]
    (edge, from_s, from_r, act, w1, w2, tile_sem, sem, out_sem) = refs[26:]
    streams = ((grad_h, grad), (normed_h, normed), (inv_h, inv), (slope_h, slope))
    leaving = ((d_pres, d_pre_h), (dxss, dxs_h), (grad_o, grad_o_h))
    got_w2 = begin(w2_h, w2, sem.at[0])
    got_w1 = begin(w1_h.at[pl.ds(0, 1024), :], w1, sem.at[1])

    def ask(i, rows):
        for k, (there, here) in enumerate(streams):
            begin(there.at[rows, :], here.at[rows, :], tile_sem.at[k, i])

    tiles(ask)
    late = [
        begin(there, here, sem.at[2 + k])
        for k, (there, here) in enumerate(
            ((edge_h, edge), (from_s_h, from_s), (from_r_h, from_r), (act_h, act))
        )
    ]
    for k, block in enumerate(blocks):
        table[pl.ds(128 * k, 128), :] = block[...]
    got_w2.wait()
    got_w1.wait()

    def tile(i, rows):
        for k, (there, here) in enumerate(streams):
            pltpu.make_async_copy(there.at[rows, :], here.at[rows, :], tile_sem.at[k, i]).wait()
        g = grad[rows, :].astype(F32) + dot(pick_rows(r_col[rows, :], 1024), table[...])
        d_out = norm_backward(g, normed[rows, :], inv[rows, :])
        d_outs[rows, :] = d_out
        d_pre = (dot_nt(d_out, w2[...]) * slope[rows, :]).astype(BF16)
        d_pres[rows, :] = d_pre
        dxss[rows, :] = dot_nt(d_pre, w1[pl.ds(512, 512), :]).astype(BF16)
        grad_o[rows, :] = (g + dot_nt(d_pre, w1[pl.ds(0, 512), :])).astype(BF16)
        for k, (here, there) in enumerate(leaving):
            begin(here.at[rows, :], there.at[rows, :], out_sem.at[k, i])

    tiles(tile)
    for k in range(4):
        sums = dot(add_rows(s_row[...], 128, 1024 + 128 * k), dxss[...])
        to = pl.ds(128 * (k // 2), 128)
        if k % 2 == 0:
            back_keep[to, :] = sums
        else:
            back_send[to, :] = sums.astype(BF16)
    mine = pl.multiple_of(core[0] * 256, 256)
    theirs = pl.multiple_of(256 - core[0] * 256, 256)
    for copy in late:
        copy.wait()
    for k, (left, right) in enumerate(
        ((d_pres, edge), (d_pres, from_s), (d_pres, from_r), (d_outs, act))
    ):
        keep_o[:, pl.ds(256 * k, 256)] = dot_tn(left[...], right[:, pl.ds(mine, 256)])
        send_o[:, pl.ds(256 * k, 256)] = dot_tn(
            left[...], right[:, pl.ds(theirs, 256)]
        ).astype(BF16)

    def finish(i, rows):
        for k, (here, there) in enumerate(leaving):
            pltpu.make_async_copy(here.at[rows, :], there.at[rows, :], out_sem.at[k, i]).wait()

    tiles(finish)


def add_kernel(keep, came, out):
    out[...] = (keep[...] + came[...].astype(F32)).astype(BF16)


def node_sums_kernel(s_row, r_row, d_pre_h, dxs_h, w1_h, out, dxr, d_pre, dxs, w_r, sem):
    got_w = begin(w1_h.at[pl.ds(1024, 512), :], w_r, sem.at[0])
    got_d = begin(d_pre_h, d_pre, sem.at[1])
    got_x = begin(dxs_h, dxs, sem.at[2])
    got_w.wait()
    got_d.wait()
    dxr[...] = dot_nt(d_pre[...], w_r[...]).astype(BF16)
    got_x.wait()
    for k in range(4):
        out[pl.ds(256 * k, 256), :] = dot(add_rows(s_row[...], 256, 256 * k), dxs[...]) + dot(
            add_rows(r_row[...], 256, 256 * k), dxr[...]
        )


def blocks_total_kernel(edge, node_h, sum_o, send_o, node, sem):
    got_n = begin(node_h, node, sem.at[0])
    edge_part = jnp.sum(edge[...].astype(F32), axis=0)
    sum_o[:, pl.ds(0, 1024)] = edge_part
    send_o[:, pl.ds(0, 1024)] = edge_part.astype(BF16)
    got_n.wait()
    node_part = jnp.sum(node[...].astype(F32), axis=0)
    sum_o[:, pl.ds(1024, 768)] = node_part
    send_o[:, pl.ds(1024, 768)] = node_part.astype(BF16)


def ring_total_kernel(own, got1, got2, got3, sum_o, send_o):
    total = own[...] + got1[...].astype(F32) + got2[...].astype(F32) + got3[...].astype(F32)
    sum_o[...] = total
    send_o[...] = total.astype(BF16)


def both_halves_kernel(core, mine, theirs, *outs):
    here = pl.multiple_of(core[0] * 256, 256)
    there = pl.multiple_of(256 - core[0] * 256, 256)
    k = 0
    for out in outs:
        for j in range(out.shape[1] // 512):
            out[:, pl.ds(512 * j + here, 256)] = mine[:, pl.ds(256 * k, 256)]
            out[:, pl.ds(512 * j + there, 256)] = theirs[:, pl.ds(256 * k, 256)].astype(F32)
            k += 1


def pair_add_kernel(keep, came, low, high):
    both = keep[...] + came[...].astype(F32)
    low[...] = both[:128].astype(BF16)
    high[...] = both[128:].astype(BF16)


def returned_kernel(index, sums, low, high, keep_o, send_o):
    for k in range(4):
        rows = (
            sums[pl.ds(256 * k, 256), :]
            + dot(add_rows(index[:, pl.ds(0, 128)], 256, 256 * k), low[...])
            + dot(add_rows(index[:, pl.ds(128, 128)], 256, 256 * k), high[...])
        )
        if k < 2:
            keep_o[pl.ds(256 * k, 256), :] = rows
        else:
            send_o[pl.ds(256 * (k - 2), 256), :] = rows.astype(BF16)


def node_total_kernel(own, got1, got2, got3, part, out):
    out[...] = (
        own[...]
        + got1[...].astype(F32)
        + got2[...].astype(F32)
        + got3[...].astype(F32)
        + part[...]
    ).astype(BF16)


def weight_sum(keep, came):
    patches = lax.axis_size("patch")
    units, lanes = keep.shape
    (both,) = call(add_kernel, [shape((units, lanes), BF16)], [keep, came], moved=4 * MIB, vmem=8 * MIB)
    return lax.all_to_all(both.reshape(patches, units // patches, lanes), "patch", 0, 0, tiled=True)


def body(
    node_latent,
    edge_latent,
    senders,
    receivers,
    halo_list,
    w_edge_first,
    w_edge_second,
    w_node_first,
    w_node_second,
    grad_node_new,
    grad_edge_new,
):
    place = lax.axis_index("shard")
    core = place & 1
    chip = place >> 1

    table_blocks = spread_over_shard(node_latent)

    def relative(n):
        return (((n >> 7) & 1) ^ core) * 512 + (((n >> 8) - chip) & 3) * 128 + (n & 127)

    s_index = jnp.where(
        senders < 256,
        1024 + ((senders >> 7) ^ core) * 128 + (senders & 127),
        jnp.where(
            senders >= 1280,
            1280 + (((senders - 1280) >> 7) ^ core) * 128 + (senders & 127),
            relative(senders - 256),
        ),
    )
    r_index = relative(receivers)
    listed = relative(halo_list[0])
    half = jnp.concatenate(
        [
            lax.dynamic_slice(listed, (core * 128,), (128,)),
            lax.dynamic_slice(listed, (256 + core * 128,), (128,)),
        ]
    )
    s_col, s_row = s_index.reshape(1024, 1), s_index.reshape(1, 1024)
    r_col, r_row = r_index.reshape(1024, 1), r_index.reshape(1, 1024)
    core_word = core.reshape(1).astype(jnp.int32)

    to_prev, to_next = call(
        halo_rows_kernel,
        [shape((128, 512), BF16)] * 2,
        [half.reshape(256, 1)] + table_blocks,
        far=(1,),
        scratch=[pltpu.VMEM((128, 512), BF16), pltpu.SemaphoreType.DMA((1,))],
        flops=2 * 256 * 1024 * 512,
        moved=2 * MIB,
        vmem=8 * MIB,
    )
    prev_mine = to_patch(to_next, 1)
    next_mine = to_patch(to_prev, -1)
    halo_blocks = [prev_mine, to_partner(prev_mine), next_mine, to_partner(next_mine)]
    from_s, from_r, pre = call(
        edge_start_kernel,
        [shape((1024, 512), BF16)] * 2 + [shape((1024, 512), F32)],
        [s_col, r_col, edge_latent] + table_blocks + [w_edge_first],
        far=(2, 3, 11),
        far_out=(1,),
        scratch=[
            pltpu.VMEM((1024, 512), BF16),
            pltpu.VMEM((1024, 512), BF16),
            pltpu.VMEM((1536, 512), BF16),
            pltpu.VMEM((1024, 512), BF16),
            pltpu.SemaphoreType.DMA((7,)),
        ],
        flops=3_800_000_000,
        moved=8 * MIB,
    )
    from_s, act, slope, normed, inv, agg_keep, agg_send = call(
        edge_forward_kernel,
        [
            shape((1024, 512), BF16),
            shape((1024, 512), BF16),
            shape((1024, 512), F32),
            shape((1024, 512), F32),
            shape((1024, 1), F32),
            shape((512, 512), F32),
            shape((512, 512), BF16),
        ],
        [s_col, r_row, edge_latent, from_s, pre] + halo_blocks + [w_edge_first, w_edge_second],
        far=(2, 9, 10),
        far_out=(0, 1, 2, 3, 4),
        scratch=[
            pltpu.VMEM((512, 512), BF16),
            pltpu.VMEM((1024, 512), BF16),
            pltpu.VMEM((1024, 512), BF16),
            pltpu.VMEM((512, 512), BF16),
            pltpu.VMEM((512, 512), BF16),
            pltpu.VMEM((1024, 512), BF16),
            pltpu.VMEM((1024, 512), BF16),
            pltpu.VMEM((1024, 512), F32),
            pltpu.VMEM((1024, 512), F32),
            pltpu.VMEM((1024, 1), F32),
            pltpu.SemaphoreType.DMA((3,)),
            pltpu.SemaphoreType.DMA((5, TILES)),
        ],
        flops=2_700_000_000,
        moved=12 * MIB,
        vmem=20 * MIB,
    )
    agg_came = to_partner(agg_send)
    agg_own, agg_1, agg_2, agg_3 = call(
        pair_sum_kernel,
        [shape((128, 512), F32)] + [shape((128, 512), BF16)] * 3,
        [agg_keep, agg_came],
        moved=2 * MIB,
        vmem=8 * MIB,
    )
    d_agg, node_part, n_keep, n_send = call(
        node_kernel,
        [
            shape((128, 512), BF16),
            shape((128, 512), F32),
            shape((512, 768), F32),
            shape((512, 768), BF16),
        ],
        [core_word, agg_own]
        + ring_sum_parts([agg_1, agg_2, agg_3])
        + [node_latent, grad_node_new, w_node_first, w_node_second],
        words=(0,),
        scratch=[pltpu.VMEM((128, 512), BF16), pltpu.VMEM((128, 512), BF16)],
        flops=800_000_000,
        moved=5 * MIB,
        vmem=8 * MIB,
    )
    d_blocks = spread_over_shard(d_agg)
    node_blocks = weight_sum(n_keep, to_partner(n_send))

    d_pre, dxs, grad_edge_latent, back_keep, back_send, w_keep, w_send = call(
        edge_backward_kernel,
        [
            shape((1024, 512), BF16),
            shape((1024, 512), BF16),
            shape((1024, 512), BF16),
            shape((256, 512), F32),
            shape((256, 512), BF16),
            shape((512, 1024), F32),
            shape((512, 1024), BF16),
        ],
        [core_word, r_col, s_row, grad_edge_new, normed, inv, slope, edge_latent, from_s, from_r, act]
        + d_blocks
        + [w_edge_first, w_edge_second],
        words=(0,),
        far=(3, 4, 5, 6, 7, 8, 9, 10, 19, 20),
        far_out=(0, 1, 2),
        scratch=[pltpu.VMEM((1024, 512), BF16)] * 6
        + [
            pltpu.VMEM((1024, 512), F32),
            pltpu.VMEM((1024, 1), F32),
            pltpu.VMEM((1024, 512), F32),
        ]
        + [pltpu.VMEM((1024, 512), BF16)] * 5
        + [
            pltpu.VMEM((512, 512), BF16),
            pltpu.SemaphoreType.DMA((4, TILES)),
            pltpu.SemaphoreType.DMA((6,)),
            pltpu.SemaphoreType.DMA((3, TILES)),
        ],
        flops=5_500_000_000,
        moved=16 * MIB,
        vmem=28 * MIB,
    )
    back_prev, back_next = call(
        pair_add_kernel,
        [shape((128, 512), BF16)] * 2,
        [back_keep, to_partner(back_send)],
        moved=MIB,
        vmem=8 * MIB,
    )
    got_next = to_patch(back_prev, -1)
    got_prev = to_patch(back_next, 1)
    edge_blocks = weight_sum(w_keep, to_partner(w_send))
    (sums,) = call(
        node_sums_kernel,
        [shape((1024, 512), F32)],
        [s_row, r_row, d_pre, dxs, w_edge_first],
        far=(2, 3, 4),
        scratch=[pltpu.VMEM((1024, 512), BF16)] * 3
        + [pltpu.VMEM((512, 512), BF16), pltpu.SemaphoreType.DMA((3,))],
        flops=2_700_000_000,
        moved=5 * MIB,
    )
    node_keep, node_send = call(
        returned_kernel,
        [shape((512, 512), F32), shape((512, 512), BF16)],
        [half.reshape(1, 256), sums, got_prev, got_next],
        flops=300_000_000,
        moved=4 * MIB,
        vmem=8 * MIB,
    )
    t_own, t_1, t_2, t_3 = call(
        pair_sum_kernel,
        [shape((128, 512), F32)] + [shape((128, 512), BF16)] * 3,
        [node_keep, to_partner(node_send)],
        moved=2 * MIB,
        vmem=8 * MIB,
    )
    (grad_node_latent,) = call(
        node_total_kernel,
        [shape((128, 512), BF16)],
        [t_own] + ring_sum_parts([t_1, t_2, t_3]) + [node_part],
        moved=MIB,
        vmem=8 * MIB,
    )

    w_rows, w_out = call(
        blocks_total_kernel,
        [shape((16, 1792), F32), shape((16, 1792), BF16)],
        [edge_blocks, node_blocks],
        far=(1,),
        scratch=[pltpu.VMEM((32, 16, 768), BF16), pltpu.SemaphoreType.DMA((1,))],
        moved=2 * MIB,
        vmem=8 * MIB,
    )
    w_rows, w_out = call(
        ring_total_kernel,
        [shape((16, 1792), F32), shape((16, 1792), BF16)],
        [w_rows] + ring_sum_parts([w_out] * 3),
        moved=MIB,
        vmem=4 * MIB,
    )
    rows = call(
        both_halves_kernel,
        [shape((16, lanes), F32) for lanes in (1536, 512, 1024, 512)],
        [core_word, w_rows, to_partner(w_out)],
        words=(0,),
        moved=MIB,
        vmem=4 * MIB,
    )
    return (grad_node_latent, grad_edge_latent) + tuple(r.T for r in rows)


def solution(mesh):
    split = P(("patch", "shard"), None)
    ids = P(("patch", "shard"))
    in_specs = (split, split, ids, ids, P("patch", None), P(), P(), P(), P(), split, split)
    out_specs = (split, split) + (P(None, "patch"),) * 4

    return jax.shard_map(body, mesh=mesh, in_specs=in_specs, out_specs=out_specs, check_vma=False)
```

```python
import jax
import jax.numpy as jnp
from jax import lax
from jax.experimental import pallas as pl
from jax.experimental.pallas import tpu as pltpu
from jax.sharding import PartitionSpec as P


epsilon = 1e-05
F32 = jnp.float32
BF16 = jnp.bfloat16
MIB = 1 << 20


def over_ring(x, by):
    count = lax.axis_size("shard")
    return lax.ppermute(x, "shard", [(i, (i + 2 * by) % count) for i in range(count)])


def to_partner(x):
    count = lax.axis_size("shard")
    return lax.ppermute(x, "shard", [(i, i ^ 1) for i in range(count)])


def to_patch(x, by):
    count = lax.axis_size("patch")
    return lax.ppermute(x, "patch", [(i, (i + by) % count) for i in range(count)])


def spread_over_shard(own):
    across = over_ring(own, 2)
    after = over_ring(own, -1)
    before = over_ring(own, 1)
    mine = [own, after, across, before]
    return mine + [to_partner(b) for b in mine]


def ring_sum_parts(chunks):
    return [over_ring(chunks[0], 1), over_ring(chunks[1], 2), over_ring(chunks[2], -1)]


def dot(a, b):
    return jnp.dot(a, b, preferred_element_type=F32)


def dot_nt(a, b):
    return lax.dot_general(a, b, (((1,), (1,)), ((), ())), preferred_element_type=F32)


def dot_tn(a, b):
    return lax.dot_general(a, b, (((0,), (0,)), ((), ())), preferred_element_type=F32)


def pick_rows(index_column, count, first=0):
    places = lax.broadcasted_iota(jnp.int32, (index_column.shape[0], count), 1) + first
    return jnp.where(places == index_column, 1.0, 0.0).astype(BF16)


def add_rows(index_row, count, first=0):
    places = lax.broadcasted_iota(jnp.int32, (count, index_row.shape[1]), 0) + first
    return jnp.where(places == index_row, 1.0, 0.0).astype(BF16)


def normalised(out):
    center = out - jnp.mean(out, axis=-1, keepdims=True)
    inv = lax.rsqrt(jnp.mean(center * center, axis=-1, keepdims=True) + epsilon)
    return center * inv, inv


def norm_backward(g, normed, inv):
    d = inv * (
        g
        - jnp.mean(g, axis=-1, keepdims=True)
        - normed * jnp.mean(g * normed, axis=-1, keepdims=True)
    )
    return d.astype(BF16)


def call(
    kernel, out_shapes, args, *, far=(), words=(), far_out=(), scratch=(), flops=0, moved=0, vmem=16 * MIB
):
    full = pl.BlockSpec(memory_space=pltpu.VMEM)
    hbm = pl.BlockSpec(memory_space=pltpu.HBM)
    smem = pl.BlockSpec(memory_space=pltpu.SMEM)
    in_specs = [hbm if i in far else smem if i in words else full for i in range(len(args))]
    out_specs = [hbm if i in far_out else full for i in range(len(out_shapes))]
    out_shapes = [
        pltpu.HBM(o.shape, o.dtype) if i in far_out else o for i, o in enumerate(out_shapes)
    ]
    args = [
        pltpu.with_memory_space_constraint(a, pltpu.HBM) if i in far else a
        for i, a in enumerate(args)
    ]
    return pl.pallas_call(
        kernel,
        out_shape=out_shapes,
        in_specs=in_specs,
        out_specs=out_specs,
        scratch_shapes=list(scratch),
        compiler_params=pltpu.CompilerParams(vmem_limit_bytes=vmem),
        cost_estimate=pl.CostEstimate(flops=flops, bytes_accessed=moved, transcendentals=0),
    )(*args)


def shape(dims, dtype):
    return jax.ShapeDtypeStruct(dims, dtype)


def begin(src, dst, sem):
    copy = pltpu.make_async_copy(src, dst, sem)
    copy.start()
    return copy


def halo_rows_kernel(index, own, *refs):
    blocks, (low, high, held, sem) = refs[:7], refs[7:]
    arriving = begin(own, held, sem.at[0])
    total = None
    for k, block in enumerate(blocks):
        part = dot(pick_rows(index[...], 128, 128 * (k + 1)), block[...])
        total = part if total is None else total + part
    arriving.wait()
    total = total + dot(pick_rows(index[...], 128), held[...])
    low[...] = total[:128].astype(BF16)
    high[...] = total[128:].astype(BF16)


TILE = 512
TILES = 2


def tiles(body):
    lax.fori_loop(
        0, TILES, lambda i, _: (body(i, pl.ds(pl.multiple_of(i * TILE, TILE), TILE)), 0)[1], 0
    )


def edge_start_kernel(s_col, r_col, edge_h, own_h, *refs):
    blocks = refs[:7]
    (w1_h, from_s, from_r_h, pre_o, table, edge, w1, from_r, sem) = refs[7:]
    got_own = begin(own_h, table.at[pl.ds(0, 128), :], sem.at[0])
    got_w1 = begin(w1_h, w1, sem.at[1])
    got_edge = begin(edge_h, edge, sem.at[2])
    for k, block in enumerate(blocks):
        table[pl.ds(128 * (k + 1), 128), :] = block[...]
    got_own.wait()

    def gather(i, rows):
        from_s[rows, :] = dot(pick_rows(s_col[rows, :], 1024), table[...]).astype(BF16)
        from_r[rows, :] = dot(pick_rows(r_col[rows, :], 1024), table[...]).astype(BF16)
        begin(from_r.at[rows, :], from_r_h.at[rows, :], sem.at[3 + i])

    tiles(gather)
    got_w1.wait()
    got_edge.wait()

    def multiply(i, rows):
        pre_o[rows, :] = (
            dot(edge[rows, :], w1[pl.ds(0, 512), :])
            + dot(from_s[rows, :], w1[pl.ds(512, 512), :])
            + dot(from_r[rows, :], w1[pl.ds(1024, 512), :])
        )

    tiles(multiply)

    def finish(i, rows):
        pltpu.make_async_copy(from_r.at[rows, :], from_r_h.at[rows, :], sem.at[3 + i]).wait()

    tiles(finish)


def edge_forward_kernel(s_col, r_row, edge_h, from_s, pre_i, *refs):
    blocks = refs[:4]
    (w1_h, w2_h, from_s_h, act_h, slope_h, normed_h, inv_h, keep_o, send_o) = refs[4:13]
    (table, news, edge, w1, w2, from_s_o, act_o, slope_o, normed_o, inv_o, sem, out_sem) = refs[13:]
    got_w1 = begin(w1_h.at[pl.ds(512, 512), :], w1, sem.at[0])
    got_w2 = begin(w2_h, w2, sem.at[1])
    got_edge = begin(edge_h, edge, sem.at[2])
    for k, block in enumerate(blocks):
        table[pl.ds(128 * k, 128), :] = block[...]
    got_w1.wait()
    got_w2.wait()
    got_edge.wait()
    leaving = (
        (from_s_o, from_s_h),
        (act_o, act_h),
        (slope_o, slope_h),
        (normed_o, normed_h),
        (inv_o, inv_h),
    )

    def tile(i, rows):
        halo = dot(pick_rows(s_col[rows, :], 512, 1024), table[...]).astype(BF16)
        from_s_o[rows, :] = from_s[rows, :] + halo
        pre = pre_i[rows, :] + dot(halo, w1[...])
        sig = jax.nn.sigmoid(pre)
        act = (pre * sig).astype(BF16)
        act_o[rows, :] = act
        slope_o[rows, :] = sig * (1.0 + pre * (1.0 - sig))
        normed, inv = normalised(dot(act, w2[...]))
        normed_o[rows, :] = normed
        inv_o[rows, :] = inv
        news[rows, :] = (edge[rows, :].astype(F32) + normed).astype(BF16)
        for k, (here, there) in enumerate(leaving):
            begin(here.at[rows, :], there.at[rows, :], out_sem.at[k, i])

    tiles(tile)
    keep_o[...] = dot(add_rows(r_row[...], 512), news[...])
    send_o[...] = dot(add_rows(r_row[...], 512, 512), news[...]).astype(BF16)

    def finish(i, rows):
        for k, (here, there) in enumerate(leaving):
            pltpu.make_async_copy(here.at[rows, :], there.at[rows, :], out_sem.at[k, i]).wait()

    tiles(finish)


def pair_sum_kernel(keep, came, own, one, two, three):
    both = keep[...] + came[...].astype(F32)
    own[...] = both[0:128]
    one[...] = both[128:256].astype(BF16)
    two[...] = both[256:384].astype(BF16)
    three[...] = both[384:512].astype(BF16)


def node_kernel(core, own, got1, got2, got3, node, grad, w1, w2, d_agg_o, part_o, keep_o, send_o, agg_s, act_s):
    agg = (
        own[...] + got1[...].astype(F32) + got2[...].astype(F32) + got3[...].astype(F32)
    ).astype(BF16)
    x = node[...]
    pre = dot(x, w1[pl.ds(0, 512), :]) + dot(agg, w1[pl.ds(512, 512), :])
    sig = jax.nn.sigmoid(pre)
    act = (pre * sig).astype(BF16)
    normed, inv = normalised(dot(act, w2[...]))
    g = grad[...].astype(F32)
    d_out = norm_backward(g, normed, inv)
    d_act = dot_nt(d_out, w2[...])
    d_pre = (d_act * (sig * (1.0 + pre * (1.0 - sig)))).astype(BF16)
    d_agg_o[...] = dot_nt(d_pre, w1[pl.ds(512, 512), :]).astype(BF16)
    part_o[...] = g + dot_nt(d_pre, w1[pl.ds(0, 512), :])
    agg_s[...] = agg
    act_s[...] = act
    mine = pl.multiple_of(core[0] * 256, 256)
    theirs = pl.multiple_of(256 - core[0] * 256, 256)
    for k, (left, right) in enumerate(((d_pre, node), (d_pre, agg_s), (d_out, act_s))):
        keep_o[:, pl.ds(256 * k, 256)] = dot_tn(left, right[:, pl.ds(mine, 256)])
        send_o[:, pl.ds(256 * k, 256)] = dot_tn(left, right[:, pl.ds(theirs, 256)]).astype(BF16)


def mask_kernel(index, out):
    def tile(i, rows):
        out[rows, :] = pick_rows(index[rows, :], 1024)

    tiles(tile)


def edge_backward_kernel(core, r_mask, s_row, r_row, grad_h, normed_h, inv_h, slope_h, edge_h, from_s_h, from_r_h, act_h, *refs):
    blocks = refs[:8]
    (w1_h, w2_h, grad_o_h, back_keep, back_send, keep_o, send_o, sums_o) = refs[8:16]
    (table, lefts, rights, dxss, dxrs, grad_o, grad, normed, inv, slope) = refs[16:26]
    (w1, w2, tile_sem, sem, out_sem) = refs[26:]
    streams = ((grad_h, grad), (normed_h, normed), (inv_h, inv), (slope_h, slope))
    got_block = begin(blocks[4], table.at[pl.ds(512, 128), :], sem.at[6])
    got_w2 = begin(w2_h, w2, sem.at[0])
    got_w1 = begin(w1_h, w1, sem.at[1])

    def ask(i, rows):
        for k, (there, here) in enumerate(streams):
            begin(there.at[rows, :], here.at[rows, :], tile_sem.at[k, i])

    tiles(ask)
    late = [
        begin(there, rights.at[k], sem.at[2 + k])
        for k, there in enumerate((edge_h, from_s_h, from_r_h, act_h))
    ]
    for k, block in enumerate(blocks):
        if k != 4:
            table[pl.ds(128 * k, 128), :] = block[...]
    got_w2.wait()
    got_w1.wait()
    got_block.wait()

    def tile(i, rows):
        for k, (there, here) in enumerate(streams):
            pltpu.make_async_copy(there.at[rows, :], here.at[rows, :], tile_sem.at[k, i]).wait()
        g = grad[rows, :].astype(F32) + dot(r_mask[rows, :], table[...])
        d_out = norm_backward(g, normed[rows, :], inv[rows, :])
        lefts[1, :, rows] = d_out.T
        d_pre = (dot_nt(d_out, w2[...]) * slope[rows, :]).astype(BF16)
        lefts[0, :, rows] = d_pre.T
        dxss[rows, :] = dot_nt(d_pre, w1[pl.ds(512, 512), :]).astype(BF16)
        dxrs[rows, :] = dot_nt(d_pre, w1[pl.ds(1024, 512), :]).astype(BF16)
        grad_o[rows, :] = (g + dot_nt(d_pre, w1[pl.ds(0, 512), :])).astype(BF16)
        begin(grad_o.at[rows, :], grad_o_h.at[rows, :], out_sem.at[i])

    tiles(tile)
    for k in range(4):
        sums = dot(add_rows(s_row[...], 128, 1024 + 128 * k), dxss[...])
        to = pl.ds(128 * (k // 2), 128)
        if k % 2 == 0:
            back_keep[to, :] = sums
        else:
            back_send[to, :] = sums.astype(BF16)

    def node_sums(i, rows):
        sums_o[rows, :] = dot(add_rows(s_row[...], TILE, TILE * i), dxss[...]) + dot(
            add_rows(r_row[...], TILE, TILE * i), dxrs[...]
        )

    tiles(node_sums)
    mine = pl.multiple_of(core[0] * 256, 256)
    theirs = pl.multiple_of(256 - core[0] * 256, 256)
    for copy in late:
        copy.wait()

    def product(k, carry):
        left = lefts[k // 3]
        to = pl.ds(pl.multiple_of(256 * k, 256), 256)
        keep_o[:, to] = dot(left, rights[k, :, pl.ds(mine, 256)])
        send_o[:, to] = dot(left, rights[k, :, pl.ds(theirs, 256)]).astype(BF16)
        return carry

    lax.fori_loop(0, 4, product, 0)

    def finish(i, rows):
        pltpu.make_async_copy(grad_o.at[rows, :], grad_o_h.at[rows, :], out_sem.at[i]).wait()

    tiles(finish)


def add_kernel(keep, came, out):
    out[...] = (keep[...] + came[...].astype(F32)).astype(BF16)


def blocks_total_kernel(edge, node_h, sum_o, send_o, node, sem):
    got_n = begin(node_h, node, sem.at[0])
    edge_part = jnp.sum(edge[...].astype(F32), axis=0)
    sum_o[:, pl.ds(0, 1024)] = edge_part
    send_o[:, pl.ds(0, 1024)] = edge_part.astype(BF16)
    got_n.wait()
    node_part = jnp.sum(node[...].astype(F32), axis=0)
    sum_o[:, pl.ds(1024, 768)] = node_part
    send_o[:, pl.ds(1024, 768)] = node_part.astype(BF16)


def ring_total_kernel(own, got1, got2, got3, sum_o, send_o):
    total = own[...] + got1[...].astype(F32) + got2[...].astype(F32) + got3[...].astype(F32)
    sum_o[...] = total
    send_o[...] = total.astype(BF16)


def both_halves_kernel(core, mine, theirs, *outs):
    here = pl.multiple_of(core[0] * 256, 256)
    there = pl.multiple_of(256 - core[0] * 256, 256)
    k = 0
    for out in outs:
        for j in range(out.shape[1] // 512):
            out[:, pl.ds(512 * j + here, 256)] = mine[:, pl.ds(256 * k, 256)]
            out[:, pl.ds(512 * j + there, 256)] = theirs[:, pl.ds(256 * k, 256)].astype(F32)
            k += 1


def pair_add_kernel(keep, came, low, high):
    both = keep[...] + came[...].astype(F32)
    low[...] = both[:128].astype(BF16)
    high[...] = both[128:].astype(BF16)


def returned_kernel(index, sums, low, high, keep_o, send_o, both):
    both[pl.ds(0, 128), :] = low[...]
    both[pl.ds(128, 128), :] = high[...]

    def rows_at(k, first):
        at = pl.multiple_of(first + 256 * k, 256)
        return sums[pl.ds(at, 256), :] + dot(add_rows(index[...], 256, at), both[...])

    def part(k, carry):
        to = pl.ds(pl.multiple_of(256 * k, 256), 256)
        send_o[to, :] = rows_at(k, 512).astype(BF16)
        keep_o[to, :] = rows_at(k, 0)
        return carry

    lax.fori_loop(0, 2, part, 0)


def node_total_kernel(own, got1, got2, got3, part, out):
    out[...] = (
        own[...]
        + got1[...].astype(F32)
        + got2[...].astype(F32)
        + got3[...].astype(F32)
        + part[...]
    ).astype(BF16)


def weight_sum(keep, came):
    patches = lax.axis_size("patch")
    units, lanes = keep.shape
    (both,) = call(add_kernel, [shape((units, lanes), BF16)], [keep, came], moved=4 * MIB, vmem=8 * MIB)
    return lax.all_to_all(both.reshape(patches, units // patches, lanes), "patch", 0, 0, tiled=True)


def body(
    node_latent,
    edge_latent,
    senders,
    receivers,
    halo_list,
    w_edge_first,
    w_edge_second,
    w_node_first,
    w_node_second,
    grad_node_new,
    grad_edge_new,
):
    place = lax.axis_index("shard")
    core = place & 1
    chip = place >> 1

    table_blocks = spread_over_shard(node_latent)

    def relative(n):
        return (((n >> 7) & 1) ^ core) * 512 + (((n >> 8) - chip) & 3) * 128 + (n & 127)

    s_index = jnp.where(
        senders < 256,
        1024 + ((senders >> 7) ^ core) * 128 + (senders & 127),
        jnp.where(
            senders >= 1280,
            1280 + (((senders - 1280) >> 7) ^ core) * 128 + (senders & 127),
            relative(senders - 256),
        ),
    )
    r_index = relative(receivers)
    listed = relative(halo_list[0])
    half = jnp.concatenate(
        [
            lax.dynamic_slice(listed, (core * 128,), (128,)),
            lax.dynamic_slice(listed, (256 + core * 128,), (128,)),
        ]
    )
    s_col, s_row = s_index.reshape(1024, 1), s_index.reshape(1, 1024)
    r_col, r_row = r_index.reshape(1024, 1), r_index.reshape(1, 1024)
    core_word = core.reshape(1).astype(jnp.int32)

    to_prev, to_next = call(
        halo_rows_kernel,
        [shape((128, 512), BF16)] * 2,
        [half.reshape(256, 1)] + table_blocks,
        far=(1,),
        scratch=[pltpu.VMEM((128, 512), BF16), pltpu.SemaphoreType.DMA((1,))],
        flops=2 * 256 * 1024 * 512,
        moved=2 * MIB,
        vmem=8 * MIB,
    )
    prev_mine = to_patch(to_next, 1)
    next_mine = to_patch(to_prev, -1)
    halo_blocks = [prev_mine, to_partner(prev_mine), next_mine, to_partner(next_mine)]
    from_s, from_r, pre = call(
        edge_start_kernel,
        [shape((1024, 512), BF16)] * 2 + [shape((1024, 512), F32)],
        [s_col, r_col, edge_latent] + table_blocks + [w_edge_first],
        far=(2, 3, 11),
        far_out=(1,),
        scratch=[
            pltpu.VMEM((1024, 512), BF16),
            pltpu.VMEM((1024, 512), BF16),
            pltpu.VMEM((1536, 512), BF16),
            pltpu.VMEM((1024, 512), BF16),
            pltpu.SemaphoreType.DMA((3 + TILES,)),
        ],
        flops=3_800_000_000,
        moved=8 * MIB,
    )
    from_s, act, slope, normed, inv, agg_keep, agg_send = call(
        edge_forward_kernel,
        [
            shape((1024, 512), BF16),
            shape((1024, 512), BF16),
            shape((1024, 512), F32),
            shape((1024, 512), F32),
            shape((1024, 1), F32),
            shape((512, 512), F32),
            shape((512, 512), BF16),
        ],
        [s_col, r_row, edge_latent, from_s, pre] + halo_blocks + [w_edge_first, w_edge_second],
        far=(2, 9, 10),
        far_out=(0, 1, 2, 3, 4),
        scratch=[
            pltpu.VMEM((512, 512), BF16),
            pltpu.VMEM((1024, 512), BF16),
            pltpu.VMEM((1024, 512), BF16),
            pltpu.VMEM((512, 512), BF16),
            pltpu.VMEM((512, 512), BF16),
            pltpu.VMEM((1024, 512), BF16),
            pltpu.VMEM((1024, 512), BF16),
            pltpu.VMEM((1024, 512), F32),
            pltpu.VMEM((1024, 512), F32),
            pltpu.VMEM((1024, 1), F32),
            pltpu.SemaphoreType.DMA((3,)),
            pltpu.SemaphoreType.DMA((5, TILES)),
        ],
        flops=2_700_000_000,
        moved=12 * MIB,
        vmem=20 * MIB,
    )
    agg_came = to_partner(agg_send)
    agg_own, agg_1, agg_2, agg_3 = call(
        pair_sum_kernel,
        [shape((128, 512), F32)] + [shape((128, 512), BF16)] * 3,
        [agg_keep, agg_came],
        moved=2 * MIB,
        vmem=8 * MIB,
    )
    d_agg, node_part, n_keep, n_send = call(
        node_kernel,
        [
            shape((128, 512), BF16),
            shape((128, 512), F32),
            shape((512, 768), F32),
            shape((512, 768), BF16),
        ],
        [core_word, agg_own]
        + ring_sum_parts([agg_1, agg_2, agg_3])
        + [node_latent, grad_node_new, w_node_first, w_node_second],
        words=(0,),
        scratch=[pltpu.VMEM((128, 512), BF16), pltpu.VMEM((128, 512), BF16)],
        flops=800_000_000,
        moved=5 * MIB,
        vmem=8 * MIB,
    )
    d_blocks = spread_over_shard(d_agg)
    node_blocks = weight_sum(n_keep, to_partner(n_send))

    (r_mask,) = call(mask_kernel, [shape((1024, 1024), BF16)], [r_col], moved=2 * MIB, vmem=8 * MIB)
    grad_edge_latent, back_keep, back_send, w_keep, w_send, sums = call(
        edge_backward_kernel,
        [
            shape((1024, 512), BF16),
            shape((256, 512), F32),
            shape((256, 512), BF16),
            shape((512, 1024), F32),
            shape((512, 1024), BF16),
            shape((1024, 512), F32),
        ],
        [core_word, r_mask, s_row, r_row, grad_edge_new, normed, inv, slope, edge_latent, from_s, from_r, act]
        + d_blocks
        + [w_edge_first, w_edge_second],
        words=(0,),
        far=(4, 5, 6, 7, 8, 9, 10, 11, 16, 20, 21),
        far_out=(0,),
        scratch=[
            pltpu.VMEM((1024, 512), BF16),
            pltpu.VMEM((2, 512, 1024), BF16),
            pltpu.VMEM((4, 1024, 512), BF16),
        ]
        + [pltpu.VMEM((1024, 512), BF16)] * 4
        + [
            pltpu.VMEM((1024, 512), F32),
            pltpu.VMEM((1024, 1), F32),
            pltpu.VMEM((1024, 512), F32),
            pltpu.VMEM((1536, 512), BF16),
            pltpu.VMEM((512, 512), BF16),
            pltpu.SemaphoreType.DMA((4, TILES)),
            pltpu.SemaphoreType.DMA((7,)),
            pltpu.SemaphoreType.DMA((TILES,)),
        ],
        flops=8_200_000_000,
        moved=16 * MIB,
        vmem=22 * MIB,
    )
    back_prev, back_next = call(
        pair_add_kernel,
        [shape((128, 512), BF16)] * 2,
        [back_keep, to_partner(back_send)],
        moved=MIB,
        vmem=8 * MIB,
    )
    got_next = to_patch(back_prev, -1)
    got_prev = to_patch(back_next, 1)
    edge_blocks = weight_sum(w_keep, to_partner(w_send))
    node_keep, node_send = call(
        returned_kernel,
        [shape((512, 512), F32), shape((512, 512), BF16)],
        [half.reshape(1, 256), sums, got_prev, got_next],
        scratch=[pltpu.VMEM((256, 512), BF16)],
        flops=300_000_000,
        moved=4 * MIB,
        vmem=8 * MIB,
    )
    t_own, t_1, t_2, t_3 = call(
        pair_sum_kernel,
        [shape((128, 512), F32)] + [shape((128, 512), BF16)] * 3,
        [node_keep, to_partner(node_send)],
        moved=2 * MIB,
        vmem=8 * MIB,
    )
    (grad_node_latent,) = call(
        node_total_kernel,
        [shape((128, 512), BF16)],
        [t_own] + ring_sum_parts([t_1, t_2, t_3]) + [node_part],
        moved=MIB,
        vmem=8 * MIB,
    )

    w_rows, w_out = call(
        blocks_total_kernel,
        [shape((16, 1792), F32), shape((16, 1792), BF16)],
        [edge_blocks, node_blocks],
        far=(1,),
        scratch=[pltpu.VMEM((32, 16, 768), BF16), pltpu.SemaphoreType.DMA((1,))],
        moved=2 * MIB,
        vmem=8 * MIB,
    )
    w_rows, w_out = call(
        ring_total_kernel,
        [shape((16, 1792), F32), shape((16, 1792), BF16)],
        [w_rows] + ring_sum_parts([w_out] * 3),
        moved=MIB,
        vmem=4 * MIB,
    )
    rows = call(
        both_halves_kernel,
        [shape((16, lanes), F32) for lanes in (1536, 512, 1024, 512)],
        [core_word, w_rows, to_partner(w_out)],
        words=(0,),
        moved=MIB,
        vmem=4 * MIB,
    )
    return (grad_node_latent, grad_edge_latent) + tuple(r.T for r in rows)


def solution(mesh):
    split = P(("patch", "shard"), None)
    ids = P(("patch", "shard"))
    in_specs = (split, split, ids, ids, P("patch", None), P(), P(), P(), P(), split, split)
    out_specs = (split, split) + (P(None, "patch"),) * 4

    return jax.shard_map(body, mesh=mesh, in_specs=in_specs, out_specs=out_specs, check_vma=False)
```

```python
import jax
import jax.numpy as jnp
from jax import lax
from jax.experimental import pallas as pl
from jax.experimental.pallas import tpu as pltpu
from jax.sharding import PartitionSpec as P


epsilon = 1e-05
F32 = jnp.float32
BF16 = jnp.bfloat16
MIB = 1 << 20


def over_ring(x, by):
    count = lax.axis_size("shard")
    return lax.ppermute(x, "shard", [(i, (i + 2 * by) % count) for i in range(count)])


def to_partner(x):
    count = lax.axis_size("shard")
    return lax.ppermute(x, "shard", [(i, i ^ 1) for i in range(count)])


def to_patch(x, by):
    count = lax.axis_size("patch")
    return lax.ppermute(x, "patch", [(i, (i + by) % count) for i in range(count)])


def spread_over_shard(own):
    after = over_ring(own, -1)
    before = over_ring(own, 1)
    across = over_ring(own, 2)
    mine = [own, after, across, before]
    return mine + [to_partner(b) for b in mine]


def ring_sum_parts(chunks):
    return [over_ring(chunks[0], 1), over_ring(chunks[1], 2), over_ring(chunks[2], -1)]


def dot(a, b):
    return jnp.dot(a, b, preferred_element_type=F32)


def dot_nt(a, b):
    return lax.dot_general(a, b, (((1,), (1,)), ((), ())), preferred_element_type=F32)


def dot_tn(a, b):
    return lax.dot_general(a, b, (((0,), (0,)), ((), ())), preferred_element_type=F32)


def pick_rows(index_column, count, first=0):
    places = lax.broadcasted_iota(jnp.int32, (index_column.shape[0], count), 1) + first
    return jnp.where(places == index_column, 1.0, 0.0).astype(BF16)


def add_rows(index_row, count, first=0):
    places = lax.broadcasted_iota(jnp.int32, (count, index_row.shape[1]), 0) + first
    return jnp.where(places == index_row, 1.0, 0.0).astype(BF16)


def sigmoid(x):
    return 0.5 * jnp.tanh(0.5 * x) + 0.5


def normalised(out):
    center = out - jnp.mean(out, axis=-1, keepdims=True)
    inv = lax.rsqrt(jnp.mean(center * center, axis=-1, keepdims=True) + epsilon)
    return center * inv, inv


def norm_backward(g, normed, inv):
    d = inv * (
        g
        - jnp.mean(g, axis=-1, keepdims=True)
        - normed * jnp.mean(g * normed, axis=-1, keepdims=True)
    )
    return d.astype(BF16)


def call(
    kernel, out_shapes, args, *, far=(), words=(), far_out=(), scratch=(), flops=0, moved=0, vmem=16 * MIB
):
    full = pl.BlockSpec(memory_space=pltpu.VMEM)
    hbm = pl.BlockSpec(memory_space=pltpu.HBM)
    smem = pl.BlockSpec(memory_space=pltpu.SMEM)
    in_specs = [hbm if i in far else smem if i in words else full for i in range(len(args))]
    out_specs = [hbm if i in far_out else full for i in range(len(out_shapes))]
    out_shapes = [
        pltpu.HBM(o.shape, o.dtype) if i in far_out else o for i, o in enumerate(out_shapes)
    ]
    args = [
        pltpu.with_memory_space_constraint(a, pltpu.HBM) if i in far else a
        for i, a in enumerate(args)
    ]
    return pl.pallas_call(
        kernel,
        out_shape=out_shapes,
        in_specs=in_specs,
        out_specs=out_specs,
        scratch_shapes=list(scratch),
        compiler_params=pltpu.CompilerParams(vmem_limit_bytes=vmem),
        cost_estimate=pl.CostEstimate(flops=flops, bytes_accessed=moved, transcendentals=0),
    )(*args)


def shape(dims, dtype):
    return jax.ShapeDtypeStruct(dims, dtype)


def begin(src, dst, sem):
    copy = pltpu.make_async_copy(src, dst, sem)
    copy.start()
    return copy


def halo_rows_kernel(index, own, *refs):
    blocks, (low, high, table, sem) = refs[:7], refs[7:]
    arriving = begin(own, table.at[pl.ds(0, 128), :], sem.at[0])
    for k, block in enumerate(blocks):
        table[pl.ds(128 * (k + 1), 128), :] = block[...]
    mask = pick_rows(index[...], 1024)
    arriving.wait()
    total = dot(mask, table[...]).astype(BF16)
    low[...] = total[:128]
    high[...] = total[128:]


TILE = 512
TILES = 2


def tiles(body):
    lax.fori_loop(
        0, TILES, lambda i, _: (body(i, pl.ds(pl.multiple_of(i * TILE, TILE), TILE)), 0)[1], 0
    )


def edge_start_kernel(s_col, r_col, r_row, table, edge_h, w1_h, w2_h, *refs):
    (from_s, from_r_h, pre_o, halo_mask, sum_mask, edge, w1, w2, from_r, sem) = refs
    got_w1 = begin(w1_h, w1, sem.at[0])
    got_edge = begin(edge_h, edge, sem.at[1])
    got_w2 = begin(w2_h, w2, sem.at[2])

    def gather(i, rows):
        from_s[rows, :] = dot(pick_rows(s_col[rows, :], 1024), table[...]).astype(BF16)
        from_r[rows, :] = dot(pick_rows(r_col[rows, :], 1024), table[...]).astype(BF16)
        begin(from_r.at[rows, :], from_r_h.at[rows, :], sem.at[3 + i])

    tiles(gather)
    got_w1.wait()
    got_edge.wait()

    def multiply(i, rows):
        pre_o[rows, :] = (
            dot(edge[rows, :], w1[pl.ds(0, 512), :])
            + dot(from_s[rows, :], w1[pl.ds(512, 512), :])
            + dot(from_r[rows, :], w1[pl.ds(1024, 512), :])
        )
        halo_mask[rows, :] = pick_rows(s_col[rows, :], 512, 1024)
        sum_mask[rows, :] = add_rows(r_row[...], TILE, TILE * i)

    tiles(multiply)

    def finish(i, rows):
        pltpu.make_async_copy(from_r.at[rows, :], from_r_h.at[rows, :], sem.at[3 + i]).wait()

    tiles(finish)
    got_w2.wait()


def edge_forward_kernel(halo_mask, sum_mask, edge, from_s, pre_i, *refs):
    blocks = refs[:4]
    (w1, w2, from_s_h, act_h, slope_h, normed_h, inv_h, keep_o, send_o) = refs[4:13]
    (table, news, from_s_o, act_o, slope_o, normed_o, inv_o, out_sem) = refs[13:]
    for k, block in enumerate(blocks):
        table[pl.ds(128 * k, 128), :] = block[...]
    leaving = (
        (from_s_o, from_s_h),
        (act_o, act_h),
        (slope_o, slope_h),
        (normed_o, normed_h),
        (inv_o, inv_h),
    )

    def tile(i, rows):
        halo = dot(halo_mask[rows, :], table[...]).astype(BF16)
        from_s_o[rows, :] = from_s[rows, :] + halo
        pre = pre_i[rows, :] + dot(halo, w1[pl.ds(512, 512), :])
        sig = sigmoid(pre)
        act = (pre * sig).astype(BF16)
        act_o[rows, :] = act
        slope_o[rows, :] = sig * (1.0 + pre * (1.0 - sig))
        normed, inv = normalised(dot(act, w2[...]))
        normed_o[rows, :] = normed
        inv_o[rows, :] = inv
        news[rows, :] = (edge[rows, :].astype(F32) + normed).astype(BF16)
        for k, (here, there) in enumerate(leaving):
            begin(here.at[rows, :], there.at[rows, :], out_sem.at[k, i])

    tiles(tile)
    keep_o[...] = dot(sum_mask[pl.ds(0, 512), :], news[...])
    send_o[...] = dot(sum_mask[pl.ds(512, 512), :], news[...]).astype(BF16)

    def finish(i, rows):
        for k, (here, there) in enumerate(leaving):
            pltpu.make_async_copy(here.at[rows, :], there.at[rows, :], out_sem.at[k, i]).wait()

    tiles(finish)


def pair_sum_kernel(keep, came, own, one, two, three):
    both = keep[...] + came[...].astype(F32)
    own[...] = both[0:128]
    one[...] = both[128:256].astype(BF16)
    two[...] = both[256:384].astype(BF16)
    three[...] = both[384:512].astype(BF16)


def node_kernel(core, own, got1, got2, got3, node, grad, w1, w2, d_agg_o, part_o, keep_o, send_o, agg_s, act_s):
    agg = (
        own[...] + got1[...].astype(F32) + got2[...].astype(F32) + got3[...].astype(F32)
    ).astype(BF16)
    x = node[...]
    pre = dot(x, w1[pl.ds(0, 512), :]) + dot(agg, w1[pl.ds(512, 512), :])
    sig = sigmoid(pre)
    act = (pre * sig).astype(BF16)
    normed, inv = normalised(dot(act, w2[...]))
    g = grad[...].astype(F32)
    d_out = norm_backward(g, normed, inv)
    d_act = dot_nt(d_out, w2[...])
    d_pre = (d_act * (sig * (1.0 + pre * (1.0 - sig)))).astype(BF16)
    d_agg_o[...] = dot_nt(d_pre, w1[pl.ds(512, 512), :]).astype(BF16)
    part_o[...] = g + dot_nt(d_pre, w1[pl.ds(0, 512), :])
    agg_s[...] = agg
    act_s[...] = act
    mine = pl.multiple_of(core[0] * 256, 256)
    theirs = pl.multiple_of(256 - core[0] * 256, 256)
    for k, (left, right) in enumerate(((d_pre, node), (d_pre, agg_s), (d_out, act_s))):
        keep_o[:, pl.ds(256 * k, 256)] = dot_tn(left, right[:, pl.ds(mine, 256)])
        send_o[:, pl.ds(256 * k, 256)] = dot_tn(left, right[:, pl.ds(theirs, 256)]).astype(BF16)


def mask_kernel(index, w1_h, w2_h, out, w1, w2, sem):
    got_w1 = begin(w1_h, w1, sem.at[0])
    got_w2 = begin(w2_h, w2, sem.at[1])

    def tile(i, rows):
        out[rows, :] = pick_rows(index[rows, :], 1024)

    tiles(tile)
    got_w1.wait()
    got_w2.wait()


def edge_backward_kernel(core, r_mask, s_row, grad_h, normed_h, inv_h, slope_h, edge_h, from_s_h, from_r_h, act_h, *refs):
    blocks = refs[:8]
    (w1, w2, grad_o_h, dxs_h, dxr_h, back_keep, back_send, keep_o, send_o) = refs[8:17]
    (table, lefts, rights, dxss, dxrs, grad_o, grad, normed, inv, slope) = refs[17:27]
    (tile_sem, sem, out_sem) = refs[27:]
    leaving = ((grad_o, grad_o_h), (dxss, dxs_h), (dxrs, dxr_h))
    streams = ((grad_h, grad), (normed_h, normed), (inv_h, inv), (slope_h, slope))
    got_block = begin(blocks[4], table.at[pl.ds(512, 128), :], sem.at[4])

    def ask(i, rows):
        for k, (there, here) in enumerate(streams):
            begin(there.at[rows, :], here.at[rows, :], tile_sem.at[k, i])

    tiles(ask)
    late = [
        begin(there, rights.at[k], sem.at[k])
        for k, there in enumerate((edge_h, from_s_h, from_r_h, act_h))
    ]
    for k, block in enumerate(blocks):
        if k != 4:
            table[pl.ds(128 * k, 128), :] = block[...]
    got_block.wait()

    def tile(i, rows):
        came = dot(r_mask[rows, :], table[...])
        for k, (there, here) in enumerate(streams):
            pltpu.make_async_copy(there.at[rows, :], here.at[rows, :], tile_sem.at[k, i]).wait()
        g = grad[rows, :].astype(F32) + came
        d_out = norm_backward(g, normed[rows, :], inv[rows, :])
        lefts[1, :, rows] = d_out.T
        d_pre = (dot_nt(d_out, w2[...]) * slope[rows, :]).astype(BF16)
        lefts[0, :, rows] = d_pre.T
        dxss[rows, :] = dot_nt(d_pre, w1[pl.ds(512, 512), :]).astype(BF16)
        dxrs[rows, :] = dot_nt(d_pre, w1[pl.ds(1024, 512), :]).astype(BF16)
        grad_o[rows, :] = (g + dot_nt(d_pre, w1[pl.ds(0, 512), :])).astype(BF16)
        for k, (here, there) in enumerate(leaving):
            begin(here.at[rows, :], there.at[rows, :], out_sem.at[k, i])

    tiles(tile)
    for k in range(4):
        sums = dot(add_rows(s_row[...], 128, 1024 + 128 * k), dxss[...])
        to = pl.ds(128 * (k // 2), 128)
        if k % 2 == 0:
            back_keep[to, :] = sums
        else:
            back_send[to, :] = sums.astype(BF16)

    mine = pl.multiple_of(core[0] * 256, 256)
    theirs = pl.multiple_of(256 - core[0] * 256, 256)
    for copy in late:
        copy.wait()

    def product(k, carry):
        left = lefts[k // 3]
        to = pl.ds(pl.multiple_of(256 * k, 256), 256)
        keep_o[:, to] = dot(left, rights[k, :, pl.ds(mine, 256)])
        send_o[:, to] = dot(left, rights[k, :, pl.ds(theirs, 256)]).astype(BF16)
        return carry

    lax.fori_loop(0, 4, product, 0)

    def finish(i, rows):
        for k, (here, there) in enumerate(leaving):
            pltpu.make_async_copy(here.at[rows, :], there.at[rows, :], out_sem.at[k, i]).wait()

    tiles(finish)


def node_sums_kernel(s_row, r_row, dxs_h, dxr_h, out, dxs, dxr, sem):
    got_s = begin(dxs_h, dxs, sem.at[0])
    got_r = begin(dxr_h, dxr, sem.at[1])
    got_s.wait()
    got_r.wait()

    def tile(i, rows):
        out[rows, :] = dot(add_rows(s_row[...], TILE, TILE * i), dxs[...]) + dot(
            add_rows(r_row[...], TILE, TILE * i), dxr[...]
        )

    tiles(tile)


def add_kernel(keep, came, out_h, out, sem):
    def part(i, carry):
        rows = pl.ds(pl.multiple_of(i * 128, 128), 128)
        out[rows, :] = (keep[rows, :] + came[rows, :].astype(F32)).astype(BF16)
        begin(out.at[rows, :], out_h.at[rows, :], sem.at[i])
        return carry

    lax.fori_loop(0, 4, part, 0)

    def finish(i, carry):
        rows = pl.ds(pl.multiple_of(i * 128, 128), 128)
        pltpu.make_async_copy(out.at[rows, :], out_h.at[rows, :], sem.at[i]).wait()
        return carry

    lax.fori_loop(0, 4, finish, 0)


def blocks_total_kernel(edge, node_h, sum_o, send_o, node, sem):
    got_n = begin(node_h, node, sem.at[0])
    edge_part = jnp.sum(edge[...].astype(F32), axis=0)
    sum_o[:, pl.ds(0, 1024)] = edge_part
    send_o[:, pl.ds(0, 1024)] = edge_part.astype(BF16)
    got_n.wait()
    node_part = jnp.sum(node[...].astype(F32), axis=0)
    sum_o[:, pl.ds(1024, 768)] = node_part
    send_o[:, pl.ds(1024, 768)] = node_part.astype(BF16)


def ring_total_kernel(own, got1, got2, got3, sum_o, send_o):
    total = own[...] + got1[...].astype(F32) + got2[...].astype(F32) + got3[...].astype(F32)
    sum_o[...] = total
    send_o[...] = total.astype(BF16)


def both_halves_kernel(core, mine, theirs, *outs):
    here = pl.multiple_of(core[0] * 256, 256)
    there = pl.multiple_of(256 - core[0] * 256, 256)
    k = 0
    for out in outs:
        for j in range(out.shape[1] // 512):
            out[:, pl.ds(512 * j + here, 256)] = mine[:, pl.ds(256 * k, 256)]
            out[:, pl.ds(512 * j + there, 256)] = theirs[:, pl.ds(256 * k, 256)].astype(F32)
            k += 1


def pair_add_kernel(keep, came, low, high):
    both = keep[...] + came[...].astype(F32)
    low[...] = both[:128].astype(BF16)
    high[...] = both[128:].astype(BF16)


def returned_kernel(index, sums, low, high, keep_o, send_o, both):
    both[pl.ds(0, 128), :] = low[...]
    both[pl.ds(128, 128), :] = high[...]

    def rows_at(k, first):
        at = pl.multiple_of(first + 256 * k, 256)
        return sums[pl.ds(at, 256), :] + dot(add_rows(index[...], 256, at), both[...])

    def part(k, carry):
        to = pl.ds(pl.multiple_of(256 * k, 256), 256)
        send_o[to, :] = rows_at(k, 512).astype(BF16)
        keep_o[to, :] = rows_at(k, 0)
        return carry

    lax.fori_loop(0, 2, part, 0)


def node_total_kernel(own, got1, got2, got3, part, out):
    out[...] = (
        own[...]
        + got1[...].astype(F32)
        + got2[...].astype(F32)
        + got3[...].astype(F32)
        + part[...]
    ).astype(BF16)


def weight_sum(keep, came):
    patches = lax.axis_size("patch")
    units, lanes = keep.shape
    (both,) = call(
        add_kernel,
        [shape((units, lanes), BF16)],
        [keep, came],
        far_out=(0,),
        scratch=[pltpu.VMEM((units, lanes), BF16), pltpu.SemaphoreType.DMA((4,))],
        moved=4 * MIB,
        vmem=8 * MIB,
    )
    return lax.all_to_all(both.reshape(patches, units // patches, lanes), "patch", 0, 0, tiled=True)


def body(
    node_latent,
    edge_latent,
    senders,
    receivers,
    halo_list,
    w_edge_first,
    w_edge_second,
    w_node_first,
    w_node_second,
    grad_node_new,
    grad_edge_new,
):
    place = lax.axis_index("shard")
    core = place & 1
    chip = place >> 1

    table_blocks = spread_over_shard(node_latent)

    def relative(n):
        return (((n >> 7) & 1) ^ core) * 512 + (((n >> 8) - chip) & 3) * 128 + (n & 127)

    s_index = jnp.where(
        senders < 256,
        1024 + ((senders >> 7) ^ core) * 128 + (senders & 127),
        jnp.where(
            senders >= 1280,
            1280 + (((senders - 1280) >> 7) ^ core) * 128 + (senders & 127),
            relative(senders - 256),
        ),
    )
    r_index = relative(receivers)
    listed = relative(halo_list[0])
    half = jnp.concatenate(
        [
            lax.dynamic_slice(listed, (core * 128,), (128,)),
            lax.dynamic_slice(listed, (256 + core * 128,), (128,)),
        ]
    )
    s_col, s_row = s_index.reshape(1024, 1), s_index.reshape(1, 1024)
    r_col, r_row = r_index.reshape(1024, 1), r_index.reshape(1, 1024)
    core_word = core.reshape(1).astype(jnp.int32)

    to_prev, to_next, table = call(
        halo_rows_kernel,
        [shape((128, 512), BF16)] * 2 + [shape((1024, 512), BF16)],
        [half.reshape(256, 1)] + table_blocks,
        far=(1,),
        scratch=[pltpu.SemaphoreType.DMA((1,))],
        flops=2 * 256 * 1024 * 512,
        moved=2 * MIB,
        vmem=8 * MIB,
    )
    prev_mine = to_patch(to_next, 1)
    next_mine = to_patch(to_prev, -1)
    halo_blocks = [prev_mine, to_partner(prev_mine), next_mine, to_partner(next_mine)]
    from_s, from_r, pre, halo_mask, sum_mask, edge_near, w1_near, w2_near = call(
        edge_start_kernel,
        [shape((1024, 512), BF16)] * 2
        + [
            shape((1024, 512), F32),
            shape((1024, 512), BF16),
            shape((1024, 1024), BF16),
            shape((1024, 512), BF16),
            shape((1536, 512), BF16),
            shape((512, 512), BF16),
        ],
        [s_col, r_col, r_row, table, edge_latent, w_edge_first, w_edge_second],
        far=(4, 5, 6),
        far_out=(1,),
        scratch=[pltpu.VMEM((1024, 512), BF16), pltpu.SemaphoreType.DMA((3 + TILES,))],
        flops=3_800_000_000,
        moved=8 * MIB,
        vmem=10 * MIB,
    )
    from_s, act, slope, normed, inv, agg_keep, agg_send = call(
        edge_forward_kernel,
        [
            shape((1024, 512), BF16),
            shape((1024, 512), BF16),
            shape((1024, 512), F32),
            shape((1024, 512), F32),
            shape((1024, 1), F32),
            shape((512, 512), F32),
            shape((512, 512), BF16),
        ],
        [halo_mask, sum_mask, edge_near, from_s, pre] + halo_blocks + [w1_near, w2_near],
        far_out=(0, 1, 2, 3, 4),
        scratch=[
            pltpu.VMEM((512, 512), BF16),
            pltpu.VMEM((1024, 512), BF16),
            pltpu.VMEM((1024, 512), BF16),
            pltpu.VMEM((1024, 512), BF16),
            pltpu.VMEM((1024, 512), F32),
            pltpu.VMEM((1024, 512), F32),
            pltpu.VMEM((1024, 1), F32),
            pltpu.SemaphoreType.DMA((5, TILES)),
        ],
        flops=2_700_000_000,
        moved=12 * MIB,
        vmem=16 * MIB,
    )
    agg_came = to_partner(agg_send)
    agg_own, agg_1, agg_2, agg_3 = call(
        pair_sum_kernel,
        [shape((128, 512), F32)] + [shape((128, 512), BF16)] * 3,
        [agg_keep, agg_came],
        moved=2 * MIB,
        vmem=8 * MIB,
    )
    d_agg, node_part, n_keep, n_send = call(
        node_kernel,
        [
            shape((128, 512), BF16),
            shape((128, 512), F32),
            shape((512, 768), F32),
            shape((512, 768), BF16),
        ],
        [core_word, agg_own]
        + ring_sum_parts([agg_1, agg_2, agg_3])
        + [node_latent, grad_node_new, w_node_first, w_node_second],
        words=(0,),
        scratch=[pltpu.VMEM((128, 512), BF16), pltpu.VMEM((128, 512), BF16)],
        flops=800_000_000,
        moved=5 * MIB,
        vmem=8 * MIB,
    )
    d_blocks = spread_over_shard(d_agg)
    node_blocks = weight_sum(n_keep, to_partner(n_send))

    r_mask, w1_back, w2_back = call(
        mask_kernel,
        [shape((1024, 1024), BF16), shape((1536, 512), BF16), shape((512, 512), BF16)],
        [r_col, w_edge_first, w_edge_second],
        far=(1, 2),
        scratch=[pltpu.SemaphoreType.DMA((2,))],
        moved=2 * MIB,
        vmem=8 * MIB,
    )
    grad_edge_latent, dxs, dxr, back_keep, back_send, w_keep, w_send = call(
        edge_backward_kernel,
        [
            shape((1024, 512), BF16),
            shape((1024, 512), BF16),
            shape((1024, 512), BF16),
            shape((256, 512), F32),
            shape((256, 512), BF16),
            shape((512, 1024), F32),
            shape((512, 1024), BF16),
        ],
        [core_word, r_mask, s_row, grad_edge_new, normed, inv, slope, edge_latent, from_s, from_r, act]
        + d_blocks
        + [w1_back, w2_back],
        words=(0,),
        far=(3, 4, 5, 6, 7, 8, 9, 10, 15),
        far_out=(0, 1, 2),
        scratch=[
            pltpu.VMEM((1024, 512), BF16),
            pltpu.VMEM((2, 512, 1024), BF16),
            pltpu.VMEM((4, 1024, 512), BF16),
        ]
        + [pltpu.VMEM((1024, 512), BF16)] * 4
        + [
            pltpu.VMEM((1024, 512), F32),
            pltpu.VMEM((1024, 1), F32),
            pltpu.VMEM((1024, 512), F32),
            pltpu.SemaphoreType.DMA((4, TILES)),
            pltpu.SemaphoreType.DMA((5,)),
            pltpu.SemaphoreType.DMA((3, TILES)),
        ],
        flops=8_200_000_000,
        moved=16 * MIB,
        vmem=22 * MIB,
    )
    back_prev, back_next = call(
        pair_add_kernel,
        [shape((128, 512), BF16)] * 2,
        [back_keep, to_partner(back_send)],
        moved=MIB,
        vmem=8 * MIB,
    )
    got_next = to_patch(back_prev, -1)
    got_prev = to_patch(back_next, 1)
    edge_blocks = weight_sum(w_keep, to_partner(w_send))
    (sums,) = call(
        node_sums_kernel,
        [shape((1024, 512), F32)],
        [s_row, r_row, dxs, dxr],
        far=(2, 3),
        scratch=[pltpu.VMEM((1024, 512), BF16)] * 2 + [pltpu.SemaphoreType.DMA((2,))],
        flops=2_100_000_000,
        moved=4 * MIB,
        vmem=12 * MIB,
    )
    node_keep, node_send = call(
        returned_kernel,
        [shape((512, 512), F32), shape((512, 512), BF16)],
        [half.reshape(1, 256), sums, got_prev, got_next],
        scratch=[pltpu.VMEM((256, 512), BF16)],
        flops=300_000_000,
        moved=4 * MIB,
        vmem=8 * MIB,
    )
    t_own, t_1, t_2, t_3 = call(
        pair_sum_kernel,
        [shape((128, 512), F32)] + [shape((128, 512), BF16)] * 3,
        [node_keep, to_partner(node_send)],
        moved=2 * MIB,
        vmem=8 * MIB,
    )
    (grad_node_latent,) = call(
        node_total_kernel,
        [shape((128, 512), BF16)],
        [t_own] + ring_sum_parts([t_1, t_2, t_3]) + [node_part],
        moved=MIB,
        vmem=8 * MIB,
    )

    w_rows, w_out = call(
        blocks_total_kernel,
        [shape((16, 1792), F32), shape((16, 1792), BF16)],
        [edge_blocks, node_blocks],
        far=(1,),
        scratch=[pltpu.VMEM((32, 16, 768), BF16), pltpu.SemaphoreType.DMA((1,))],
        moved=2 * MIB,
        vmem=8 * MIB,
    )
    w_rows, w_out = call(
        ring_total_kernel,
        [shape((16, 1792), F32), shape((16, 1792), BF16)],
        [w_rows] + ring_sum_parts([w_out] * 3),
        moved=MIB,
        vmem=4 * MIB,
    )
    rows = call(
        both_halves_kernel,
        [shape((16, lanes), F32) for lanes in (1536, 512, 1024, 512)],
        [core_word, w_rows, to_partner(w_out)],
        words=(0,),
        moved=MIB,
        vmem=4 * MIB,
    )
    return (grad_node_latent, grad_edge_latent) + tuple(r.T for r in rows)


def solution(mesh):
    split = P(("patch", "shard"), None)
    ids = P(("patch", "shard"))
    in_specs = (split, split, ids, ids, P("patch", None), P(), P(), P(), P(), split, split)
    out_specs = (split, split) + (P(None, "patch"),) * 4

    return jax.shard_map(body, mesh=mesh, in_specs=in_specs, out_specs=out_specs, check_vma=False)
```

```python
import jax
import jax.numpy as jnp
from jax import lax
from jax.experimental import pallas as pl
from jax.experimental.pallas import tpu as pltpu
from jax.sharding import PartitionSpec as P


epsilon = 1e-05
F32 = jnp.float32
BF16 = jnp.bfloat16
MIB = 1 << 20


def over_ring(x, by):
    count = lax.axis_size("shard")
    return lax.ppermute(x, "shard", [(i, (i + 2 * by) % count) for i in range(count)])


def to_partner(x):
    count = lax.axis_size("shard")
    return lax.ppermute(x, "shard", [(i, i ^ 1) for i in range(count)])


def to_patch(x, by):
    count = lax.axis_size("patch")
    return lax.ppermute(x, "patch", [(i, (i + by) % count) for i in range(count)])


def spread_over_shard(own):
    after = over_ring(own, -1)
    before = over_ring(own, 1)
    across = over_ring(own, 2)
    mine = [own, after, across, before]
    return mine + [to_partner(b) for b in mine]


def ring_sum_parts(chunks):
    return [over_ring(chunks[0], 1), over_ring(chunks[1], 2), over_ring(chunks[2], -1)]


def dot(a, b):
    return jnp.dot(a, b, preferred_element_type=F32)


def dot_nt(a, b):
    return lax.dot_general(a, b, (((1,), (1,)), ((), ())), preferred_element_type=F32)


def dot_tn(a, b):
    return lax.dot_general(a, b, (((0,), (0,)), ((), ())), preferred_element_type=F32)


def pick_rows(index_column, count, first=0):
    places = lax.broadcasted_iota(jnp.int32, (index_column.shape[0], count), 1) + first
    return jnp.where(places == index_column, 1.0, 0.0).astype(BF16)


def add_rows(index_row, count, first=0):
    places = lax.broadcasted_iota(jnp.int32, (count, index_row.shape[1]), 0) + first
    return jnp.where(places == index_row, 1.0, 0.0).astype(BF16)


def sigmoid(x):
    return 0.5 * jnp.tanh(0.5 * x) + 0.5


def normalised(out):
    center = out - jnp.mean(out, axis=-1, keepdims=True)
    inv = lax.rsqrt(jnp.mean(center * center, axis=-1, keepdims=True) + epsilon)
    return center * inv, inv


def norm_backward(g, normed, inv):
    d = inv * (
        g
        - jnp.mean(g, axis=-1, keepdims=True)
        - normed * jnp.mean(g * normed, axis=-1, keepdims=True)
    )
    return d.astype(BF16)


def call(
    kernel, out_shapes, args, *, far=(), words=(), far_out=(), scratch=(), flops=0, moved=0, vmem=16 * MIB
):
    full = pl.BlockSpec(memory_space=pltpu.VMEM)
    hbm = pl.BlockSpec(memory_space=pltpu.HBM)
    smem = pl.BlockSpec(memory_space=pltpu.SMEM)
    in_specs = [hbm if i in far else smem if i in words else full for i in range(len(args))]
    out_specs = [hbm if i in far_out else full for i in range(len(out_shapes))]
    out_shapes = [
        pltpu.HBM(o.shape, o.dtype) if i in far_out else o for i, o in enumerate(out_shapes)
    ]
    args = [
        pltpu.with_memory_space_constraint(a, pltpu.HBM) if i in far else a
        for i, a in enumerate(args)
    ]
    return pl.pallas_call(
        kernel,
        out_shape=out_shapes,
        in_specs=in_specs,
        out_specs=out_specs,
        scratch_shapes=list(scratch),
        compiler_params=pltpu.CompilerParams(vmem_limit_bytes=vmem),
        cost_estimate=pl.CostEstimate(flops=flops, bytes_accessed=moved, transcendentals=0),
    )(*args)


def shape(dims, dtype):
    return jax.ShapeDtypeStruct(dims, dtype)


def begin(src, dst, sem):
    copy = pltpu.make_async_copy(src, dst, sem)
    copy.start()
    return copy


def halo_rows_kernel(index, own, *refs):
    blocks, (low, high, table, sem) = refs[:7], refs[7:]
    arriving = begin(own, table.at[pl.ds(0, 128), :], sem.at[0])
    for k, block in enumerate(blocks):
        table[pl.ds(128 * (k + 1), 128), :] = block[...]
    mask = pick_rows(index[...], 1024)
    arriving.wait()
    total = dot(mask, table[...]).astype(BF16)
    low[...] = total[:128]
    high[...] = total[128:]


TILE = 512
TILES = 2


def tiles(body):
    lax.fori_loop(
        0, TILES, lambda i, _: (body(i, pl.ds(pl.multiple_of(i * TILE, TILE), TILE)), 0)[1], 0
    )


def edge_start_kernel(s_col, r_col, r_row, table, edge_h, w1_h, w2_h, *refs):
    (from_s, from_r_h, pre_o, halo_mask, sum_mask, edge, w1, w2, from_r, sem) = refs
    got_w1 = begin(w1_h, w1, sem.at[0])
    got_edge = begin(edge_h, edge, sem.at[1])
    got_w2 = begin(w2_h, w2, sem.at[2])

    def gather(i, rows):
        from_s[rows, :] = dot(pick_rows(s_col[rows, :], 1024), table[...]).astype(BF16)
        from_r[rows, :] = dot(pick_rows(r_col[rows, :], 1024), table[...]).astype(BF16)
        begin(from_r.at[rows, :], from_r_h.at[rows, :], sem.at[3 + i])

    tiles(gather)
    got_w1.wait()
    got_edge.wait()

    def multiply(i, rows):
        pre_o[rows, :] = (
            dot(edge[rows, :], w1[pl.ds(0, 512), :])
            + dot(from_s[rows, :], w1[pl.ds(512, 512), :])
            + dot(from_r[rows, :], w1[pl.ds(1024, 512), :])
        )
        halo_mask[rows, :] = pick_rows(s_col[rows, :], 512, 1024)
        sum_mask[rows, :] = add_rows(r_row[...], TILE, TILE * i)

    tiles(multiply)

    def finish(i, rows):
        pltpu.make_async_copy(from_r.at[rows, :], from_r_h.at[rows, :], sem.at[3 + i]).wait()

    tiles(finish)
    got_w2.wait()


def edge_forward_kernel(halo_mask, sum_mask, edge, from_s, pre_i, *refs):
    blocks = refs[:4]
    (w1, w2, from_s_h, act_h, slope_h, normed_h, inv_h, keep_o, send_o) = refs[4:13]
    (table, news, from_s_o, act_o, slope_o, normed_o, inv_o, out_sem) = refs[13:]
    for k, block in enumerate(blocks):
        table[pl.ds(128 * k, 128), :] = block[...]
    leaving = (
        (from_s_o, from_s_h),
        (act_o, act_h),
        (slope_o, slope_h),
        (normed_o, normed_h),
        (inv_o, inv_h),
    )

    def tile(i, rows):
        halo = dot(halo_mask[rows, :], table[...]).astype(BF16)
        from_s_o[rows, :] = from_s[rows, :] + halo
        pre = pre_i[rows, :] + dot(halo, w1[pl.ds(512, 512), :])
        sig = sigmoid(pre)
        act = (pre * sig).astype(BF16)
        act_o[rows, :] = act
        slope_o[rows, :] = sig * (1.0 + pre * (1.0 - sig))
        normed, inv = normalised(dot(act, w2[...]))
        normed_o[rows, :] = normed
        inv_o[rows, :] = inv
        news[rows, :] = (edge[rows, :].astype(F32) + normed).astype(BF16)
        for k, (here, there) in enumerate(leaving):
            begin(here.at[rows, :], there.at[rows, :], out_sem.at[k, i])

    tiles(tile)
    keep_o[...] = dot(sum_mask[pl.ds(0, 512), :], news[...])
    send_o[...] = dot(sum_mask[pl.ds(512, 512), :], news[...]).astype(BF16)

    def finish(i, rows):
        for k, (here, there) in enumerate(leaving):
            pltpu.make_async_copy(here.at[rows, :], there.at[rows, :], out_sem.at[k, i]).wait()

    tiles(finish)


def pair_sum_kernel(keep, came, own, one, two, three):
    both = keep[...] + came[...].astype(F32)
    own[...] = both[0:128]
    one[...] = both[128:256].astype(BF16)
    two[...] = both[256:384].astype(BF16)
    three[...] = both[384:512].astype(BF16)


def node_kernel(core, own, got1, got2, got3, node, grad, w1, w2, d_agg_o, part_o, keep_o, send_o, agg_s, act_s):
    agg = (
        own[...] + got1[...].astype(F32) + got2[...].astype(F32) + got3[...].astype(F32)
    ).astype(BF16)
    x = node[...]
    pre = dot(x, w1[pl.ds(0, 512), :]) + dot(agg, w1[pl.ds(512, 512), :])
    sig = sigmoid(pre)
    act = (pre * sig).astype(BF16)
    normed, inv = normalised(dot(act, w2[...]))
    g = grad[...].astype(F32)
    d_out = norm_backward(g, normed, inv)
    d_act = dot_nt(d_out, w2[...])
    d_pre = (d_act * (sig * (1.0 + pre * (1.0 - sig)))).astype(BF16)
    d_agg_o[...] = dot_nt(d_pre, w1[pl.ds(512, 512), :]).astype(BF16)
    part_o[...] = g + dot_nt(d_pre, w1[pl.ds(0, 512), :])
    agg_s[...] = agg
    act_s[...] = act
    mine = pl.multiple_of(core[0] * 256, 256)
    theirs = pl.multiple_of(256 - core[0] * 256, 256)
    for k, (left, right) in enumerate(((d_pre, node), (d_pre, agg_s), (d_out, act_s))):
        keep_o[:, pl.ds(256 * k, 256)] = dot_tn(left, right[:, pl.ds(mine, 256)])
        send_o[:, pl.ds(256 * k, 256)] = dot_tn(left, right[:, pl.ds(theirs, 256)]).astype(BF16)


def mask_kernel(index, w1_h, w2_h, out, w1, w2, sem):
    got_w1 = begin(w1_h, w1, sem.at[0])
    got_w2 = begin(w2_h, w2, sem.at[1])

    def tile(i, rows):
        out[rows, :] = pick_rows(index[rows, :], 1024)

    tiles(tile)
    got_w1.wait()
    got_w2.wait()


def edge_backward_kernel(core, r_mask, s_row, grad_h, normed_h, inv_h, slope_h, edge_h, from_s_h, from_r_h, act_h, *refs):
    blocks = refs[:8]
    (w1, w2, grad_o_h, dxs_h, dxr_h, back_keep, back_send, keep_o, send_o) = refs[8:17]
    (table, lefts, rights, dxss, dxrs, grad_o, grad, normed, inv, slope) = refs[17:27]
    (tile_sem, sem, out_sem) = refs[27:]
    leaving = ((grad_o, grad_o_h), (dxss, dxs_h), (dxrs, dxr_h))
    streams = ((grad_h, grad), (normed_h, normed), (inv_h, inv), (slope_h, slope))
    got_block = begin(blocks[4], table.at[pl.ds(512, 128), :], sem.at[4])

    def ask(i, rows):
        for k, (there, here) in enumerate(streams):
            begin(there.at[rows, :], here.at[rows, :], tile_sem.at[k, i])

    tiles(ask)
    late = [
        begin(there, rights.at[k], sem.at[k])
        for k, there in enumerate((edge_h, from_s_h, from_r_h, act_h))
    ]
    for k, block in enumerate(blocks):
        if k != 4:
            table[pl.ds(128 * k, 128), :] = block[...]
    got_block.wait()

    def tile(i, rows):
        came = dot(r_mask[rows, :], table[...])
        for k, (there, here) in enumerate(streams):
            pltpu.make_async_copy(there.at[rows, :], here.at[rows, :], tile_sem.at[k, i]).wait()
        g = grad[rows, :].astype(F32) + came
        d_out = norm_backward(g, normed[rows, :], inv[rows, :])
        lefts[1, :, rows] = d_out.T
        d_pre = (dot_nt(d_out, w2[...]) * slope[rows, :]).astype(BF16)
        lefts[0, :, rows] = d_pre.T
        dxss[rows, :] = dot_nt(d_pre, w1[pl.ds(512, 512), :]).astype(BF16)
        dxrs[rows, :] = dot_nt(d_pre, w1[pl.ds(1024, 512), :]).astype(BF16)
        grad_o[rows, :] = (g + dot_nt(d_pre, w1[pl.ds(0, 512), :])).astype(BF16)
        for k, (here, there) in enumerate(leaving):
            begin(here.at[rows, :], there.at[rows, :], out_sem.at[k, i])

    tiles(tile)
    for k in range(4):
        sums = dot(add_rows(s_row[...], 128, 1024 + 128 * k), dxss[...])
        to = pl.ds(128 * (k // 2), 128)
        if k % 2 == 0:
            back_keep[to, :] = sums
        else:
            back_send[to, :] = sums.astype(BF16)

    mine = pl.multiple_of(core[0] * 256, 256)
    theirs = pl.multiple_of(256 - core[0] * 256, 256)
    for copy in late:
        copy.wait()

    def product(k, carry):
        left = lefts[k // 3]
        to = pl.ds(pl.multiple_of(256 * k, 256), 256)
        keep_o[:, to] = dot(left, rights[k, :, pl.ds(mine, 256)])
        send_o[:, to] = dot(left, rights[k, :, pl.ds(theirs, 256)]).astype(BF16)
        return carry

    lax.fori_loop(0, 4, product, 0)

    def finish(i, rows):
        for k, (here, there) in enumerate(leaving):
            pltpu.make_async_copy(here.at[rows, :], there.at[rows, :], out_sem.at[k, i]).wait()

    tiles(finish)


def node_sums_kernel(s_row, r_row, dxs_h, dxr_h, out, dxs, dxr, sem):
    got_s = begin(dxs_h, dxs, sem.at[0])
    got_r = begin(dxr_h, dxr, sem.at[1])
    got_s.wait()
    got_r.wait()

    def tile(i, rows):
        out[rows, :] = dot(add_rows(s_row[...], TILE, TILE * i), dxs[...]) + dot(
            add_rows(r_row[...], TILE, TILE * i), dxr[...]
        )

    tiles(tile)


def add_kernel(keep, came, out_h, out, sem):
    def part(i, carry):
        rows = pl.ds(pl.multiple_of(i * 128, 128), 128)
        out[rows, :] = (keep[rows, :] + came[rows, :].astype(F32)).astype(BF16)
        begin(out.at[rows, :], out_h.at[rows, :], sem.at[i])
        return carry

    lax.fori_loop(0, 4, part, 0)

    def finish(i, carry):
        rows = pl.ds(pl.multiple_of(i * 128, 128), 128)
        pltpu.make_async_copy(out.at[rows, :], out_h.at[rows, :], sem.at[i]).wait()
        return carry

    lax.fori_loop(0, 4, finish, 0)


def node_blocks_kernel(node_h, out, node, sem):
    begin(node_h, node, sem.at[0]).wait()
    out[...] = jnp.sum(node[...].astype(F32), axis=0)


def blocks_total_kernel(edge, node_part, sum_o, send_o):
    edge_part = jnp.sum(edge[...].astype(F32), axis=0)
    sum_o[:, pl.ds(0, 1024)] = edge_part
    send_o[:, pl.ds(0, 1024)] = edge_part.astype(BF16)
    sum_o[:, pl.ds(1024, 768)] = node_part[...]
    send_o[:, pl.ds(1024, 768)] = node_part[...].astype(BF16)


def ring_total_kernel(own, got1, got2, got3, sum_o, send_o):
    total = own[...] + got1[...].astype(F32) + got2[...].astype(F32) + got3[...].astype(F32)
    sum_o[...] = total
    send_o[...] = total.astype(BF16)


def both_halves_kernel(core, mine, theirs, *outs):
    here = pl.multiple_of(core[0] * 256, 256)
    there = pl.multiple_of(256 - core[0] * 256, 256)
    k = 0
    for out in outs:
        for j in range(out.shape[1] // 512):
            out[:, pl.ds(512 * j + here, 256)] = mine[:, pl.ds(256 * k, 256)]
            out[:, pl.ds(512 * j + there, 256)] = theirs[:, pl.ds(256 * k, 256)].astype(F32)
            k += 1


def pair_add_kernel(keep, came, low, high):
    both = keep[...] + came[...].astype(F32)
    low[...] = both[:128].astype(BF16)
    high[...] = both[128:].astype(BF16)


def returned_kernel(index, sums, low, high, keep_o, send_o, both):
    both[pl.ds(0, 128), :] = low[...]
    both[pl.ds(128, 128), :] = high[...]

    def rows_at(k, first):
        at = pl.multiple_of(first + 256 * k, 256)
        return sums[pl.ds(at, 256), :] + dot(add_rows(index[...], 256, at), both[...])

    def part(k, carry):
        to = pl.ds(pl.multiple_of(256 * k, 256), 256)
        send_o[to, :] = rows_at(k, 512).astype(BF16)
        keep_o[to, :] = rows_at(k, 0)
        return carry

    lax.fori_loop(0, 2, part, 0)


def node_total_kernel(own, got1, got2, got3, part, out):
    out[...] = (
        own[...]
        + got1[...].astype(F32)
        + got2[...].astype(F32)
        + got3[...].astype(F32)
        + part[...]
    ).astype(BF16)


def weight_sum(keep, came):
    patches = lax.axis_size("patch")
    units, lanes = keep.shape
    (both,) = call(
        add_kernel,
        [shape((units, lanes), BF16)],
        [keep, came],
        far_out=(0,),
        scratch=[pltpu.VMEM((units, lanes), BF16), pltpu.SemaphoreType.DMA((4,))],
        moved=4 * MIB,
        vmem=8 * MIB,
    )
    return lax.all_to_all(both.reshape(patches, units // patches, lanes), "patch", 0, 0, tiled=True)


def body(
    node_latent,
    edge_latent,
    senders,
    receivers,
    halo_list,
    w_edge_first,
    w_edge_second,
    w_node_first,
    w_node_second,
    grad_node_new,
    grad_edge_new,
):
    place = lax.axis_index("shard")
    core = place & 1
    chip = place >> 1

    table_blocks = spread_over_shard(node_latent)

    def relative(n):
        return (((n >> 7) & 1) ^ core) * 512 + (((n >> 8) - chip) & 3) * 128 + (n & 127)

    s_index = jnp.where(
        senders < 256,
        1024 + ((senders >> 7) ^ core) * 128 + (senders & 127),
        jnp.where(
            senders >= 1280,
            1280 + (((senders - 1280) >> 7) ^ core) * 128 + (senders & 127),
            relative(senders - 256),
        ),
    )
    r_index = relative(receivers)
    listed = relative(halo_list[0])
    half = jnp.concatenate(
        [
            lax.dynamic_slice(listed, (core * 128,), (128,)),
            lax.dynamic_slice(listed, (256 + core * 128,), (128,)),
        ]
    )
    s_col, s_row = s_index.reshape(1024, 1), s_index.reshape(1, 1024)
    r_col, r_row = r_index.reshape(1024, 1), r_index.reshape(1, 1024)
    core_word = core.reshape(1).astype(jnp.int32)

    to_prev, to_next, table = call(
        halo_rows_kernel,
        [shape((128, 512), BF16)] * 2 + [shape((1024, 512), BF16)],
        [half.reshape(256, 1)] + table_blocks,
        far=(1,),
        scratch=[pltpu.SemaphoreType.DMA((1,))],
        flops=2 * 256 * 1024 * 512,
        moved=2 * MIB,
        vmem=8 * MIB,
    )
    prev_mine = to_patch(to_next, 1)
    next_mine = to_patch(to_prev, -1)
    halo_blocks = [prev_mine, to_partner(prev_mine), next_mine, to_partner(next_mine)]
    from_s, from_r, pre, halo_mask, sum_mask, edge_near, w1_near, w2_near = call(
        edge_start_kernel,
        [shape((1024, 512), BF16)] * 2
        + [
            shape((1024, 512), F32),
            shape((1024, 512), BF16),
            shape((1024, 1024), BF16),
            shape((1024, 512), BF16),
            shape((1536, 512), BF16),
            shape((512, 512), BF16),
        ],
        [s_col, r_col, r_row, table, edge_latent, w_edge_first, w_edge_second],
        far=(4, 5, 6),
        far_out=(1,),
        scratch=[pltpu.VMEM((1024, 512), BF16), pltpu.SemaphoreType.DMA((3 + TILES,))],
        flops=3_800_000_000,
        moved=8 * MIB,
        vmem=10 * MIB,
    )
    from_s, act, slope, normed, inv, agg_keep, agg_send = call(
        edge_forward_kernel,
        [
            shape((1024, 512), BF16),
            shape((1024, 512), BF16),
            shape((1024, 512), F32),
            shape((1024, 512), F32),
            shape((1024, 1), F32),
            shape((512, 512), F32),
            shape((512, 512), BF16),
        ],
        [halo_mask, sum_mask, edge_near, from_s, pre] + halo_blocks + [w1_near, w2_near],
        far_out=(0, 1, 2, 3, 4),
        scratch=[
            pltpu.VMEM((512, 512), BF16),
            pltpu.VMEM((1024, 512), BF16),
            pltpu.VMEM((1024, 512), BF16),
            pltpu.VMEM((1024, 512), BF16),
            pltpu.VMEM((1024, 512), F32),
            pltpu.VMEM((1024, 512), F32),
            pltpu.VMEM((1024, 1), F32),
            pltpu.SemaphoreType.DMA((5, TILES)),
        ],
        flops=2_700_000_000,
        moved=12 * MIB,
        vmem=16 * MIB,
    )
    agg_came = to_partner(agg_send)
    agg_own, agg_1, agg_2, agg_3 = call(
        pair_sum_kernel,
        [shape((128, 512), F32)] + [shape((128, 512), BF16)] * 3,
        [agg_keep, agg_came],
        moved=2 * MIB,
        vmem=8 * MIB,
    )
    d_agg, node_part, n_keep, n_send = call(
        node_kernel,
        [
            shape((128, 512), BF16),
            shape((128, 512), F32),
            shape((512, 768), F32),
            shape((512, 768), BF16),
        ],
        [core_word, agg_own]
        + ring_sum_parts([agg_1, agg_2, agg_3])
        + [node_latent, grad_node_new, w_node_first, w_node_second],
        words=(0,),
        scratch=[pltpu.VMEM((128, 512), BF16), pltpu.VMEM((128, 512), BF16)],
        flops=800_000_000,
        moved=5 * MIB,
        vmem=8 * MIB,
    )
    d_blocks = spread_over_shard(d_agg)
    node_blocks = weight_sum(n_keep, to_partner(n_send))

    r_mask, w1_back, w2_back = call(
        mask_kernel,
        [shape((1024, 1024), BF16), shape((1536, 512), BF16), shape((512, 512), BF16)],
        [r_col, w_edge_first, w_edge_second],
        far=(1, 2),
        scratch=[pltpu.SemaphoreType.DMA((2,))],
        moved=2 * MIB,
        vmem=8 * MIB,
    )
    grad_edge_latent, dxs, dxr, back_keep, back_send, w_keep, w_send = call(
        edge_backward_kernel,
        [
            shape((1024, 512), BF16),
            shape((1024, 512), BF16),
            shape((1024, 512), BF16),
            shape((256, 512), F32),
            shape((256, 512), BF16),
            shape((512, 1024), F32),
            shape((512, 1024), BF16),
        ],
        [core_word, r_mask, s_row, grad_edge_new, normed, inv, slope, edge_latent, from_s, from_r, act]
        + d_blocks
        + [w1_back, w2_back],
        words=(0,),
        far=(3, 4, 5, 6, 7, 8, 9, 10, 15),
        far_out=(0, 1, 2),
        scratch=[
            pltpu.VMEM((1024, 512), BF16),
            pltpu.VMEM((2, 512, 1024), BF16),
            pltpu.VMEM((4, 1024, 512), BF16),
        ]
        + [pltpu.VMEM((1024, 512), BF16)] * 4
        + [
            pltpu.VMEM((1024, 512), F32),
            pltpu.VMEM((1024, 1), F32),
            pltpu.VMEM((1024, 512), F32),
            pltpu.SemaphoreType.DMA((4, TILES)),
            pltpu.SemaphoreType.DMA((5,)),
            pltpu.SemaphoreType.DMA((3, TILES)),
        ],
        flops=8_200_000_000,
        moved=16 * MIB,
        vmem=22 * MIB,
    )
    back_prev, back_next = call(
        pair_add_kernel,
        [shape((128, 512), BF16)] * 2,
        [back_keep, to_partner(back_send)],
        moved=MIB,
        vmem=8 * MIB,
    )
    got_next = to_patch(back_prev, -1)
    got_prev = to_patch(back_next, 1)
    edge_blocks = weight_sum(w_keep, to_partner(w_send))
    (sums,) = call(
        node_sums_kernel,
        [shape((1024, 512), F32)],
        [s_row, r_row, dxs, dxr],
        far=(2, 3),
        scratch=[pltpu.VMEM((1024, 512), BF16)] * 2 + [pltpu.SemaphoreType.DMA((2,))],
        flops=2_100_000_000,
        moved=4 * MIB,
        vmem=12 * MIB,
    )
    node_keep, node_send = call(
        returned_kernel,
        [shape((512, 512), F32), shape((512, 512), BF16)],
        [half.reshape(1, 256), sums, got_prev, got_next],
        scratch=[pltpu.VMEM((256, 512), BF16)],
        flops=300_000_000,
        moved=4 * MIB,
        vmem=8 * MIB,
    )
    t_own, t_1, t_2, t_3 = call(
        pair_sum_kernel,
        [shape((128, 512), F32)] + [shape((128, 512), BF16)] * 3,
        [node_keep, to_partner(node_send)],
        moved=2 * MIB,
        vmem=8 * MIB,
    )
    (grad_node_latent,) = call(
        node_total_kernel,
        [shape((128, 512), BF16)],
        [t_own] + ring_sum_parts([t_1, t_2, t_3]) + [node_part],
        moved=MIB,
        vmem=8 * MIB,
    )

    (node_sum,) = call(
        node_blocks_kernel,
        [shape((16, 768), F32)],
        [node_blocks],
        far=(0,),
        scratch=[pltpu.VMEM((32, 16, 768), BF16), pltpu.SemaphoreType.DMA((1,))],
        moved=MIB,
        vmem=4 * MIB,
    )
    w_rows, w_out = call(
        blocks_total_kernel,
        [shape((16, 1792), F32), shape((16, 1792), BF16)],
        [edge_blocks, node_sum],
        moved=MIB,
        vmem=4 * MIB,
    )
    w_rows, w_out = call(
        ring_total_kernel,
        [shape((16, 1792), F32), shape((16, 1792), BF16)],
        [w_rows] + ring_sum_parts([w_out] * 3),
        moved=MIB,
        vmem=4 * MIB,
    )
    rows = call(
        both_halves_kernel,
        [shape((16, lanes), F32) for lanes in (1536, 512, 1024, 512)],
        [core_word, w_rows, to_partner(w_out)],
        words=(0,),
        moved=MIB,
        vmem=4 * MIB,
    )
    return (grad_node_latent, grad_edge_latent) + tuple(r.T for r in rows)


def solution(mesh):
    split = P(("patch", "shard"), None)
    ids = P(("patch", "shard"))
    in_specs = (split, split, ids, ids, P("patch", None), P(), P(), P(), P(), split, split)
    out_specs = (split, split) + (P(None, "patch"),) * 4

    return jax.shard_map(body, mesh=mesh, in_specs=in_specs, out_specs=out_specs, check_vma=False)
```
